256 devices in a mesh: group: 16 (over z, core), shard: 16 (over y, x).
Axes of the slice: x: 4, y: 4, z: 8, core: 2. Of those that a mesh axis runs over, the one named last changes fastest.
Arguments:
- tokens: bfloat16 [512, 1280], P(('group', 'shard')), as said below
- kv_cache: bfloat16 [512, 128, 2560], P(('group', 'shard'))
- keep_list: int32 [512, 128], P(('group', 'shard')), may hold values from 0 to 1
- lengths: int32 [512], P(('group', 'shard')), may hold values from 64 to 128
- merge_index: int32 [512, 128], P(('group', 'shard')), may hold values from 0 to 15
- merge_table: bfloat16 [16], replicated, may hold values from 0.0099487305 to 0.099609375
- move_offset: int32 [16, 2], P('shard'), may hold values from 0 to 15, as said below
- pair_mask: int32 [16], P('shard'), may hold values from 1 to 15
- w_qkv: bfloat16 [1280, 3840], P(None, 'shard'), may hold values from -0.15625 to 0.15625
- w_out: bfloat16 [1280, 1280], P(None, 'shard'), may hold values from -0.15625 to 0.15625
- w_up: bfloat16 [1280, 5120], P(None, 'shard'), may hold values from -0.15625 to 0.15625
- w_gate: bfloat16 [1280, 5120], P(None, 'shard'), may hold values from -0.15625 to 0.15625
- w_down: bfloat16 [5120, 1280], P('shard'), may hold values from -0.078125 to 0.078125
- qk_scale: float32 [1280], replicated, may hold values from 0.5 to 2
- attn_rate: float32 [1280], replicated, may hold values from 0.05 to 0.5
- mlp_rate: float32 [1280], replicated, may hold values from 0.05 to 0.5
- up_scale: float32 [5120], P('shard'), may hold values from 0.5 to 2
- gate_scale: float32 [5120], P('shard'), may hold values from 0.5 to 2
Outputs:
- new_hidden: bfloat16 [512, 1280], P(('group', 'shard'))
- moved_cache: bfloat16 [512, 128, 2560], P(('group', 'shard'))
The draws below stay inside these ranges and needn't reach their ends.
Inputs may be any that keep to these rules, and one draw needn't show every extreme that they name: `tokens`: slot 1 of group g and shard s holds the same token as that slot of group g XOR pair_mask[s] on shard s. `move_offset`: the 2 offsets of one shard index are distinct.
All inputs are finite; a program needn't handle non-finite values.
Results may differ from the reference program's by a relative error of at most 0.011.
Values may be sent and summed in bfloat16 or wider, within the bound.
A program may use at most 128 MiB of HBM per device.

```python
import math
import jax
import jax.numpy as jnp
from jax import lax

D = 1280
DH = 64
HEADS = 20
FF = 5120
RQ = 2
CTX = 128
BLOCK = 128
NBLK = 1
WTAB = 16
SLOTS = 512
N_GROUP = 16
N_SHARD = 16


def pair_bits(key):
    values = jax.random.randint(jax.random.fold_in(key, 11), (N_SHARD,), 1, N_GROUP, dtype=jnp.int32)
    position = jax.random.randint(jax.random.fold_in(key, 12), (), 0, N_SHARD, dtype=jnp.int32)
    values = values.at[position].set(N_GROUP - 1)
    if N_SHARD > 1:
        distance = jax.random.randint(jax.random.fold_in(key, 13), (), 1, N_SHARD, dtype=jnp.int32)
        values = values.at[(position + distance) % N_SHARD].set(1)
    return values


def draw_pair_mask(key, part):
    return pair_bits(key)


def draw_tokens(key, part):
    pair_masks = pair_bits(key)
    base_rows = jax.random.normal(jax.random.fold_in(key, 1), (N_GROUP, N_SHARD, RQ, D), jnp.float32)
    groups = jnp.arange(N_GROUP, dtype=jnp.int32)[:, None]
    lower_group = jnp.minimum(groups, jnp.bitwise_xor(groups, pair_masks[None, :]))
    shards = jnp.broadcast_to(jnp.arange(N_SHARD, dtype=jnp.int32)[None, :], (N_GROUP, N_SHARD))
    paired = base_rows[lower_group, shards, RQ - 1]
    base_rows = base_rows.at[:, :, RQ - 1].set(paired)
    return base_rows.reshape(SLOTS, D).astype(jnp.bfloat16)


def draw_kv_cache(key, part):
    key_rows = 0.15 * jax.random.normal(jax.random.fold_in(key, 1), (SLOTS, CTX, D), jnp.float32)
    value_rows = jax.random.normal(jax.random.fold_in(key, 2), (SLOTS, CTX, D), jnp.float32)
    return jnp.concatenate([key_rows, value_rows], axis=-1).astype(jnp.bfloat16)


def draw_keep_list(key, part):
    keep_rates = jax.random.randint(jax.random.fold_in(key, 1), (SLOTS, NBLK, 1), 3, 8)
    draw_picks = jax.random.randint(jax.random.fold_in(key, 2), (SLOTS, NBLK, BLOCK), 0, 8)
    return (draw_picks < keep_rates).astype(jnp.int32).reshape(SLOTS, CTX)


def draw_move_offset(key, part):
    scores = jax.random.randint(key, (N_SHARD, N_GROUP), 0, 2 ** 20) * N_GROUP + jnp.arange(N_GROUP, dtype=jnp.int32)[None, :]
    scores = scores.at[0, N_GROUP - 1].set(-1)
    ranking = jnp.argsort(scores, axis=1)
    return ranking[:, :RQ].astype(jnp.int32)


def place_ends(values, stream_key, smallest, largest):
    extent = values.shape
    place = [jax.random.randint(jax.random.fold_in(stream_key, axis), (), 0, extent[axis]) for axis in range(len(extent))]
    values = values.at[tuple(place)].set(smallest)
    longest = extent.index(max(extent))
    place[longest] = (place[longest] + 1) % extent[longest]
    return values.at[tuple(place)].set(largest)


def block_scale(own_key, shape, cuts, least, top_value):
    loudness = 1.0
    for axis_at, parts in cuts:
        draws = jax.random.uniform(jax.random.fold_in(jax.random.fold_in(own_key, 6), axis_at), (parts,), jnp.float32, least / len(cuts), top_value / len(cuts))
        loudness = loudness * jnp.repeat(jnp.exp(draws), shape[axis_at] // parts).reshape((-1,) + (1,) * (len(shape) - 1 - axis_at))
    return loudness


def gaussian(key, shape, scale, limit, split=(), held_as=jnp.bfloat16):
    level = block_scale(key, shape, split, -0.22, 0.18) if split else 1.0
    values = jax.random.normal(key, shape, jnp.float32) * scale * level
    return jnp.minimum(jnp.maximum(values, -limit), limit).astype(held_as)


def setup_inputs(seed: int = 0) -> dict:
    splits = jax.random.split(jax.random.key(seed), 19)
    tokens = draw_tokens(jax.random.fold_in(splits[18], 71), 0)
    kv_cache = draw_kv_cache(jax.random.fold_in(splits[18], 71), 0)
    keep_list = draw_keep_list(jax.random.fold_in(splits[18], 71), 0)
    lengths = place_ends(jax.random.randint(splits[3], (SLOTS,), CTX // 2, CTX + 1), jax.random.fold_in(splits[3], 1), CTX // 2, CTX).astype(jnp.int32)
    merge_index = place_ends(jax.random.randint(splits[4], (SLOTS, CTX), 0, WTAB), jax.random.fold_in(splits[4], 1), 0, WTAB - 1).astype(jnp.int32)
    merge_table = jnp.clip(jnp.exp(jax.random.uniform(splits[5], (WTAB,), jnp.float32, math.log(0.0099487305), math.log(0.099609375))), 0.0099487305, 0.099609375).astype(jnp.bfloat16)
    move_offset = draw_move_offset(jax.random.fold_in(splits[18], 71), 0)
    pair_mask = draw_pair_mask(jax.random.fold_in(splits[18], 71), 0)
    w_qkv = gaussian(splits[8], (D, 3 * D), D ** -0.5, 0.15625, ((1, 16),))
    w_out = gaussian(splits[9], (D, D), D ** -0.5, 0.15625, ((1, 16),))
    w_up = gaussian(splits[10], (D, FF), D ** -0.5, 0.15625, ((1, 16),))
    w_gate = gaussian(splits[11], (D, FF), D ** -0.5, 0.15625, ((1, 16),))
    w_down = gaussian(splits[12], (FF, D), FF ** -0.5, 0.078125, ((0, 16),))
    qk_scale = jnp.clip(jnp.exp(jax.random.uniform(splits[13], (D,), jnp.float32, math.log(0.5), math.log(2.0))), 0.5, 2.0)
    attn_rate = jnp.clip(jnp.exp(jax.random.uniform(splits[14], (D,), jnp.float32, math.log(0.05), math.log(0.5))), 0.05, 0.5)
    mlp_rate = jnp.clip(jnp.exp(jax.random.uniform(splits[15], (D,), jnp.float32, math.log(0.05), math.log(0.5))), 0.05, 0.5)
    up_scale = jnp.clip(jnp.exp(math.log(2.0) - 1.3862944 * jax.random.uniform(splits[16], (FF,), jnp.float32) ** block_scale(splits[16], (FF,), ((0, 16),), -0.2, 0.2)), 0.5, 2.0)
    gate_scale = jnp.clip(jnp.exp(math.log(2.0) - 1.3862944 * jax.random.uniform(splits[17], (FF,), jnp.float32) ** block_scale(splits[17], (FF,), ((0, 16),), -0.2, 0.2)), 0.5, 2.0)
    return dict(tokens=tokens, kv_cache=kv_cache, keep_list=keep_list, lengths=lengths, merge_index=merge_index, merge_table=merge_table, move_offset=move_offset, pair_mask=pair_mask, w_qkv=w_qkv, w_out=w_out, w_up=w_up, w_gate=w_gate, w_down=w_down, qk_scale=qk_scale, attn_rate=attn_rate, mlp_rate=mlp_rate, up_scale=up_scale, gate_scale=gate_scale)


EPSILON = 1e-06
NEGATIVE = -1e+30

def rms_normal(vector):
    return vector * lax.rsqrt(lax.optimization_barrier(jnp.mean(vector * vector, axis=-1, keepdims=True)) + EPSILON)

def head_normal(vector, scaling):
    return vector * lax.rsqrt(lax.optimization_barrier(jnp.sum(vector * vector, axis=-1, keepdims=True)) + EPSILON) * scaling

def rounded(vector):
    return lax.optimization_barrier(vector.astype(jnp.bfloat16)).astype(jnp.float32)

def compact_block(block_rows, keep_row, valid_row, index_row, merge_table):
    keeper = (keep_row == 1) & valid_row
    dropper = (keep_row == 0) & valid_row
    position = jnp.cumsum(keeper.astype(jnp.int32), dtype=jnp.int32) - 1
    kept_count = jnp.sum(keeper.astype(jnp.int32), dtype=jnp.int32)
    drop_count = jnp.sum(dropper.astype(jnp.int32), dtype=jnp.int32)
    target = jnp.arange(BLOCK, dtype=jnp.int32)
    placing = jnp.where((position[None, :] == target[:, None]) & keeper[None, :], 1.0, 0.0).astype(jnp.float32)
    weights = merge_table.astype(jnp.float32)[index_row] * dropper.astype(jnp.float32)
    summing = jnp.where(target[:, None] == kept_count, 1.0, 0.0).astype(jnp.float32) * weights[None, :]
    mixing = placing + summing
    result = jnp.dot(mixing, block_rows.astype(jnp.float32), precision=lax.Precision.HIGHEST)
    return (result.astype(jnp.bfloat16), kept_count + (drop_count > 0).astype(jnp.int32))

def reference(tokens, kv_cache, keep_list, lengths, merge_index, merge_table, move_offset, pair_mask, w_qkv, w_out, w_up, w_gate, w_down, qk_scale, attn_rate, mlp_rate, up_scale, gate_scale):

    def compact_slot(arguments):
        cache_rows, keep_row, length, index_row = arguments
        in_length = jnp.arange(CTX, dtype=jnp.int32) < length

        def one_block(block_rows, block_keep, block_valid, block_index):
            return compact_block(block_rows, block_keep, block_valid, block_index, merge_table)
        packed, live_count = jax.vmap(one_block)(cache_rows.reshape(NBLK, BLOCK, 2 * D), keep_row.reshape(NBLK, BLOCK), in_length.reshape(NBLK, BLOCK), index_row.reshape(NBLK, BLOCK))
        return (packed.reshape(CTX, 2 * D), live_count)
    compacted, live_count = lax.map(compact_slot, (kv_cache, keep_list, lengths, merge_index))
    group_ids = jnp.arange(N_GROUP, dtype=jnp.int32)[:, None, None]
    shard_ids = jnp.arange(N_SHARD, dtype=jnp.int32)[None, :, None]
    slot_ids = jnp.arange(RQ, dtype=jnp.int32)[None, None, :]
    source_group = (group_ids - move_offset[None, :, :]) % N_GROUP
    source = ((source_group * N_SHARD + shard_ids) * RQ + slot_ids).reshape(SLOTS)
    moved_cache = compacted[source]
    moved_live = live_count[source]
    projected = jnp.dot(tokens, w_qkv, preferred_element_type=jnp.float32).astype(jnp.bfloat16)
    head_scale = qk_scale.reshape(HEADS, DH)
    queries = head_normal(projected[:, :D].astype(jnp.float32).reshape(SLOTS, HEADS, DH), head_scale).astype(jnp.bfloat16)
    new_keys = head_normal(projected[:, D:2 * D].astype(jnp.float32).reshape(SLOTS, HEADS, DH), head_scale).astype(jnp.bfloat16)
    new_values = projected[:, 2 * D:].reshape(SLOTS, HEADS, DH)
    slot_all = jnp.arange(SLOTS, dtype=jnp.int32)
    group_of = slot_all // (N_SHARD * RQ)
    shard_of = slot_all // RQ % N_SHARD
    within = slot_all % RQ
    partner_group = jnp.bitwise_xor(group_of, pair_mask[shard_of])
    is_long = within == RQ - 1
    include = jnp.logical_not(is_long) | (group_of < partner_group)
    partner = (partner_group * N_SHARD + shard_of) * RQ + within
    score_scale = float(DH) ** 0.5

    def attend(arguments):
        query_row, new_key, new_value, cache_rows, live_row, with_new = arguments
        key_rows = cache_rows[:, :D].astype(jnp.float32).reshape(CTX, HEADS, DH)
        value_rows = cache_rows[:, D:].astype(jnp.float32).reshape(CTX, HEADS, DH)
        query_wide = query_row.astype(jnp.float32)
        scores = score_scale * jnp.einsum('hd,rhd->hr', query_wide, key_rows, precision=lax.Precision.HIGHEST)
        fresh_score = score_scale * lax.optimization_barrier(jnp.sum(query_wide * new_key.astype(jnp.float32), axis=-1))
        row_valid = jnp.arange(CTX, dtype=jnp.int32) % BLOCK < jnp.repeat(live_row, BLOCK)
        highest = jnp.maximum(lax.optimization_barrier(jnp.max(jnp.where(row_valid[None, :], scores, NEGATIVE), axis=1)), jnp.where(with_new, fresh_score, NEGATIVE))
        safe_scores = jnp.where(row_valid[None, :], scores, highest[:, None])
        soft_weights = jnp.where(row_valid[None, :], jnp.exp(safe_scores - highest[:, None]), 0.0)
        fresh_weight = jnp.where(with_new, jnp.exp(fresh_score - highest), 0.0)
        weight_sum = lax.optimization_barrier(jnp.sum(soft_weights, axis=1)) + fresh_weight
        weighted = jnp.einsum('hr,rhd->hd', rounded(soft_weights), value_rows, precision=lax.Precision.HIGHEST)
        weighted = weighted + rounded(fresh_weight)[:, None] * new_value.astype(jnp.float32)
        return (highest, weight_sum, weighted)
    highest, weight_sum, weighted = lax.map(attend, (queries, new_keys, new_values, moved_cache, moved_live, include))
    other_high = highest[partner]
    other_sum = weight_sum[partner]
    other_weighted = weighted[partner]
    merged = jnp.maximum(highest, other_high)
    own_factor = jnp.exp(highest - merged)
    other_factor = jnp.exp(other_high - merged)
    long_sum = weight_sum * own_factor + other_sum * other_factor
    long_weighted = weighted * own_factor[:, :, None] + other_weighted * other_factor[:, :, None]
    weight_sum = jnp.where(is_long[:, None], long_sum, weight_sum)
    weighted = jnp.where(is_long[:, None, None], long_weighted, weighted)
    attended = (weighted / weight_sum[:, :, None]).reshape(SLOTS, D).astype(jnp.bfloat16)
    attention_out = jnp.dot(attended, w_out, preferred_element_type=jnp.float32).astype(jnp.bfloat16)
    hidden = tokens.astype(jnp.float32)
    mixed = rms_normal(hidden + attn_rate * (rms_normal(attention_out.astype(jnp.float32)) - hidden))
    mixed_low = mixed.astype(jnp.bfloat16)
    up_part = jnp.dot(mixed_low, w_up, preferred_element_type=jnp.float32) * up_scale
    gate_part = jnp.dot(mixed_low, w_gate, preferred_element_type=jnp.float32) * (gate_scale * float(D) ** 0.5)
    inner = (up_part * jax.nn.silu(gate_part)).astype(jnp.bfloat16)
    mlp_out = jnp.dot(inner, w_down, preferred_element_type=jnp.float32)
    new_hidden = rms_normal(mixed + mlp_rate * (rms_normal(mlp_out) - mixed)).astype(jnp.bfloat16)
    return (new_hidden, moved_cache)
```

```python
import functools
import math

import jax
import jax.numpy as jnp
from jax import lax
from jax.experimental import pallas as pl
from jax.experimental.pallas import tpu as pltpu
from jax.sharding import PartitionSpec as P

DH = 64
WTAB = 16
N = 16
D = 1280
HEADS_PAD = 32
EPSILON = 1e-06
NEGATIVE = -1e30
MESH = pl.DeviceIdType.MESH
F32 = jnp.float32
BF16 = jnp.bfloat16


def iota(shape, axis):
    return lax.broadcasted_iota(jnp.int32, shape, axis)


def rms_normal(vector):
    return vector * lax.rsqrt(jnp.mean(vector * vector, axis=-1, keepdims=True) + EPSILON)


def wait_for(ref, sem):
    pltpu.make_async_copy(ref, ref, sem).wait()


def layer_kernel(
    lengths,
    offsets,
    pair_bits,
    keep_ref,
    index_ref,
    table_ref,
    qk_ref,
    attn_rate_ref,
    mlp_rate_ref,
    up_scale_ref,
    gate_scale_ref,
    tokens_hbm,
    kv_hbm,
    w_qkv_hbm,
    w_out_hbm,
    w_up_hbm,
    w_gate_hbm,
    w_down_hbm,
    hidden_out,
    cache_out,
    kv,
    w_qkv,
    w_out,
    w_up,
    w_gate,
    w_down,
    packed,
    arrived,
    staged,
    group_rows,
    shard_rows,
    lhs,
    qkv_send,
    qkv_recv,
    qkv_flat,
    partial,
    attended_rows,
    out_send,
    out_recv,
    out_flat,
    mixed_rows,
    sum_wide,
    sum_send,
    sum_recv,
    local_sem,
    send_sem,
    recv_sem,
):
    my_group = lax.axis_index("group")
    my_shard = lax.axis_index("shard")

    def group_peer(k):
        return (lax.rem(my_group + k, N), my_shard)

    def shard_peer(k):
        return (my_group, lax.rem(my_shard + k, N))

    loads = []
    for number, (source, target) in enumerate(
        (
            (tokens_hbm, group_rows.at[0]),
            (kv_hbm, kv),
            (w_qkv_hbm, w_qkv),
            (w_out_hbm, w_out),
            (w_up_hbm, w_up),
            (w_gate_hbm, w_gate),
            (w_down_hbm, w_down),
        )
    ):
        copy = pltpu.make_async_copy(source, target, local_sem.at[number])
        copy.start()
        loads.append(copy)

    barrier = pltpu.get_barrier_semaphore()

    def greet(k, carry):
        pl.semaphore_signal(barrier, inc=1, device_id=group_peer(k), device_id_type=MESH)
        pl.semaphore_signal(barrier, inc=1, device_id=shard_peer(k), device_id_type=MESH)
        return carry

    lax.fori_loop(1, N, greet, 0)

    def push(source, target, peer, hop):
        def one(k, carry):
            pltpu.make_async_remote_copy(
                src_ref=source(k),
                dst_ref=target(k),
                send_sem=send_sem.at[hop],
                recv_sem=recv_sem.at[hop],
                device_id=peer(k),
                device_id_type=MESH,
            ).start()
            return carry

        lax.fori_loop(1, N, one, 0)

    def others(ref):
        return ref.at[pl.ds(1, N - 1)]

    def gather(rows, peer, hop):
        push(lambda k: rows.at[0], lambda k: rows.at[k], peer, hop)

    def give_back(source, target, hop):
        push(lambda k: source.at[k], lambda k: target.at[k], lambda k: shard_peer(N - k), hop)

    loads[0].wait()
    pl.semaphore_wait(barrier, 2 * (N - 1))

    gather(group_rows, group_peer, 0)

    rows2 = iota((2, 128), 0)
    lane = iota((1, 128), 1)
    length2 = jnp.where(rows2 == 0, lengths[0], lengths[1])
    in_length = iota((2, 128), 1) < length2
    keeper = jnp.where((keep_ref[...] == 1) & in_length, 1.0, 0.0)
    dropper = jnp.where((keep_ref[...] == 0) & in_length, 1.0, 0.0)
    lower = jnp.where(iota((128, 128), 0) <= iota((128, 128), 1), 1.0, 0.0).astype(BF16)
    position = jnp.dot(keeper.astype(BF16), lower, preferred_element_type=F32)
    place2 = jnp.where(keeper > 0.0, position - 1.0, -1.0)
    kept = jnp.sum(keeper, axis=1, keepdims=True)
    live2 = kept + jnp.where(jnp.sum(dropper, axis=1, keepdims=True) > 0.0, 1.0, 0.0)
    table_square = jnp.broadcast_to(table_ref[...].astype(F32), (WTAB, WTAB))
    table_column = jnp.sum(
        jnp.where(iota((WTAB, WTAB), 0) == iota((WTAB, WTAB), 1), table_square, 0.0),
        axis=1,
        keepdims=True,
    )
    target_row = iota((128, 128), 0).astype(F32)
    loads[1].wait()
    for j in range(2):
        hit = iota((WTAB, 128), 0) == index_ref[j : j + 1, :]
        weights = (
            jnp.sum(jnp.where(hit, table_column, 0.0), axis=0, keepdims=True)
            * dropper[j : j + 1, :]
        )
        placing = jnp.where(target_row == place2[j : j + 1, :], 1.0, 0.0)
        summing = jnp.where(target_row == kept[j : j + 1, :], weights, 0.0)
        mixing = (placing + summing).astype(BF16)
        for block in range(5):
            columns = slice(512 * block, 512 * block + 512)
            result = jnp.dot(mixing, kv[j, :, columns], preferred_element_type=F32)
            packed[8 * j : 8 * j + 8, :, columns] = result.astype(BF16).reshape(8, 16, 512)

    push(
        lambda k: packed.at[lax.rem(my_group + k, N)],
        lambda k: arrived.at[k],
        group_peer,
        1,
    )
    arrived[0] = packed[my_group]

    wait_for(others(group_rows), recv_sem.at[0])
    offset0 = offsets[0, 0]
    offset1 = offsets[0, 1]
    first = iota((2, D), 0) == 0
    own_tokens = group_rows[0].astype(F32)
    moved_tokens = jnp.where(
        first,
        group_rows[lax.rem(N - offset0, N)].astype(F32),
        group_rows[lax.rem(N - offset1, N)].astype(F32),
    )
    shard_rows[0] = moved_tokens.astype(BF16)
    gather(shard_rows, shard_peer, 2)

    def stack(rows):
        for k in range(N):
            lhs[2 * k : 2 * k + 2, :] = rows[k].astype(F32)
        return lhs[...].astype(BF16)

    def shifter(width, frame):
        shift = lax.rem(width * my_shard, 128)
        return jnp.where(
            iota((width, frame), 1) == iota((width, frame), 0) + shift, 1.0, 0.0
        ).astype(BF16)

    def spread_back(rows, weight, width, frame, send, recv, flat, hop):
        columns = jnp.dot(rows, weight, preferred_element_type=F32).astype(BF16)
        framed = jnp.dot(columns, shifter(width, frame), preferred_element_type=F32)
        for k in range(N):
            send[k] = framed[2 * k : 2 * k + 2, :]
        recv[0] = framed[0:2, :]
        give_back(send, recv, hop)
        flat[...] = jnp.zeros(flat.shape, F32)
        wait_for(others(recv), recv_sem.at[hop])
        for c in range(N):
            begin = 128 * ((width * c) // 128)
            flat[:, begin : begin + frame] += recv[lax.rem(c + N - my_shard, N)]

    loads[2].wait()
    wait_for(others(shard_rows), recv_sem.at[2])
    spread_back(stack(shard_rows), w_qkv[...], 240, 384, qkv_send, qkv_recv, qkv_flat, 3)

    head_mask = lax.shift_right_logical(iota((HEADS_PAD, D), 1), 6) == iota((HEADS_PAD, D), 0)
    eye = iota((HEADS_PAD, 128), 0) == iota((HEADS_PAD, 128), 1)
    scaling = qk_ref[...]
    score_scale = float(DH) ** 0.5

    def heads(row):
        masked = jnp.where(head_mask, jnp.broadcast_to(row, (HEADS_PAD, D)), 0.0)
        squares = jnp.sum(masked * masked, axis=1, keepdims=True)
        return (masked * lax.rsqrt(squares + EPSILON) * scaling).astype(BF16)

    home = lax.rem(my_group + offset1, N)
    partner_here = jnp.bitwise_xor(home, pair_bits[0])
    for j in range(2):
        queries = heads(qkv_flat[j : j + 1, 0:D])
        new_keys = heads(qkv_flat[j : j + 1, D : 2 * D])
        new_values = qkv_flat[j : j + 1, 2 * D : 3 * D]
        keys = packed[8 * j : 8 * j + 8, :, 0:D].reshape(128, D)
        values = packed[8 * j : 8 * j + 8, :, D : 2 * D].reshape(128, D)
        scores = score_scale * lax.dot_general(
            queries, keys, (((1,), (1,)), ((), ())), preferred_element_type=F32
        )
        fresh = score_scale * jnp.sum(
            queries.astype(F32) * new_keys.astype(F32), axis=1, keepdims=True
        )
        if j == 1:
            counted = jnp.full((HEADS_PAD, 1), home, jnp.int32) < partner_here
        else:
            counted = jnp.full((HEADS_PAD, 1), True)
        valid = jnp.broadcast_to(lane.astype(F32) < live2[j : j + 1, :], (HEADS_PAD, 128))
        highest = jnp.maximum(
            jnp.max(jnp.where(valid, scores, NEGATIVE), axis=1, keepdims=True),
            jnp.where(counted, fresh, NEGATIVE),
        )
        soft = jnp.where(valid, jnp.exp(jnp.where(valid, scores - highest, 0.0)), 0.0)
        fresh_weight = jnp.where(counted, jnp.exp(fresh - highest), 0.0)
        weight_sum = jnp.sum(soft, axis=1, keepdims=True) + fresh_weight
        weighted = jnp.dot(soft.astype(BF16), values, preferred_element_type=F32)
        weighted = weighted + fresh_weight.astype(BF16).astype(F32) * new_values
        if j == 0:
            weighted = weighted / weight_sum
        partial[0, :, j * D : j * D + D] = jnp.sum(
            jnp.where(head_mask, weighted, 0.0), axis=0, keepdims=True
        )
        if j == 1:
            partial[0, :, 2 * D : 2 * D + 128] = jnp.sum(
                jnp.where(eye, highest, 0.0), axis=0, keepdims=True
            )
            partial[0, :, 2 * D + 128 : 2 * D + 256] = jnp.sum(
                jnp.where(eye, weight_sum, 0.0), axis=0, keepdims=True
            )

    gather(partial, group_peer, 4)

    wait_for(others(arrived), recv_sem.at[1])
    my_offset = offsets[0, lax.div(my_group, 8)]
    for m in range(N):
        staged[m] = arrived[lax.rem(my_offset + N - m, N)]
    landing = cache_out.at[
        lax.div(my_group, 8), pl.ds(pl.multiple_of(16 * lax.rem(my_group, 8), 16), 16), :
    ]
    push(lambda k: staged.at[k], lambda k: landing, group_peer, 5)
    own_chunk = pltpu.make_async_copy(staged.at[0], landing, local_sem.at[7])
    own_chunk.start()

    wait_for(others(partial), recv_sem.at[4])
    partner = jnp.bitwise_xor(my_group, pair_bits[0])
    mine = partial[offset1]
    other = partial[lax.rem(my_group - partner + offset1 + N, N)]
    my_high = mine[:, 2 * D : 2 * D + 128]
    other_high = other[:, 2 * D : 2 * D + 128]
    merged = jnp.maximum(my_high, other_high)
    my_factor = jnp.exp(my_high - merged)
    other_factor = jnp.exp(other_high - merged)
    long_sum = (
        mine[:, 2 * D + 128 : 2 * D + 256] * my_factor
        + other[:, 2 * D + 128 : 2 * D + 256] * other_factor
    )

    def by_column(row):
        column = jnp.sum(
            jnp.where(eye, jnp.broadcast_to(row, (HEADS_PAD, 128)), 0.0), axis=1, keepdims=True
        )
        return jnp.sum(jnp.where(head_mask, column, 0.0), axis=0, keepdims=True)

    long_row = mine[:, D : 2 * D] * by_column(my_factor / long_sum) + other[
        :, D : 2 * D
    ] * by_column(other_factor / long_sum)
    short_row = partial[offset0][:, 0:D]
    attended = jnp.where(
        first, jnp.broadcast_to(short_row, (2, D)), jnp.broadcast_to(long_row, (2, D))
    )
    attended_rows[0] = attended.astype(BF16)
    gather(attended_rows, shard_peer, 6)

    loads[3].wait()
    wait_for(others(attended_rows), recv_sem.at[6])
    spread_back(stack(attended_rows), w_out[...], 80, 256, out_send, out_recv, out_flat, 7)
    attention_out = out_flat[:, 0:D]
    mixed = rms_normal(
        own_tokens + attn_rate_ref[...] * (rms_normal(attention_out) - own_tokens)
    )
    mixed_rows[0] = mixed.astype(BF16)
    gather(mixed_rows, shard_peer, 8)

    loads[4].wait()
    loads[5].wait()
    loads[6].wait()
    wait_for(others(mixed_rows), recv_sem.at[8])
    rows = stack(mixed_rows)
    up = jnp.dot(rows, w_up[...], preferred_element_type=F32) * up_scale_ref[...]
    gate = jnp.dot(rows, w_gate[...], preferred_element_type=F32) * (
        gate_scale_ref[...] * float(D) ** 0.5
    )
    inner = (up * (gate / (1.0 + jnp.exp(-gate)))).astype(BF16)
    sum_wide[...] = jnp.dot(inner, w_down[...], preferred_element_type=F32)
    for k in range(N):
        sum_send[k] = sum_wide[2 * k : 2 * k + 2, :].astype(BF16)
    sum_recv[0] = sum_send[0]
    give_back(sum_send, sum_recv, 9)
    wait_for(others(sum_recv), recv_sem.at[9])
    mlp_out = sum_recv[0].astype(F32)
    for k in range(1, N):
        mlp_out = mlp_out + sum_recv[k].astype(F32)
    hidden_out[...] = rms_normal(
        mixed + mlp_rate_ref[...] * (rms_normal(mlp_out) - mixed)
    ).astype(BF16)

    fifteen = pl.ds(1, N - 1)
    wait_for(others(staged), recv_sem.at[5])
    own_chunk.wait()
    for hop, ref in enumerate(
        (
            group_rows,
            arrived,
            shard_rows,
            qkv_recv,
            partial,
            staged,
            attended_rows,
            out_recv,
            mixed_rows,
            sum_recv,
        )
    ):
        wait_for(others(ref), send_sem.at[hop])


def per_device(
    tokens,
    kv_cache,
    keep_list,
    lengths,
    merge_index,
    merge_table,
    move_offset,
    pair_mask,
    w_qkv,
    w_out,
    w_up,
    w_gate,
    w_down,
    qk_scale,
    attn_rate,
    mlp_rate,
    up_scale,
    gate_scale,
):
    smem = pl.BlockSpec(memory_space=pltpu.SMEM)
    vmem = pl.BlockSpec(memory_space=pltpu.VMEM)
    anywhere = pl.BlockSpec(memory_space=pl.ANY)

    def row(vector):
        return vector.reshape(1, -1)

    return pl.pallas_call(
        layer_kernel,
        out_shape=(
            jax.ShapeDtypeStruct((2, D), BF16),
            jax.ShapeDtypeStruct((2, 128, 2 * D), BF16),
        ),
        in_specs=[smem] * 3 + [vmem] * 8 + [anywhere] * 7,
        out_specs=(vmem, anywhere),
        scratch_shapes=[
            pltpu.VMEM((2, 128, 2 * D), BF16),
            pltpu.VMEM((D, 240), BF16),
            pltpu.VMEM((D, 80), BF16),
            pltpu.VMEM((D, 320), BF16),
            pltpu.VMEM((D, 320), BF16),
            pltpu.VMEM((320, D), BF16),
            pltpu.VMEM((N, 16, 2 * D), BF16),
            pltpu.VMEM((N, 16, 2 * D), BF16),
            pltpu.VMEM((N, 16, 2 * D), BF16),
            pltpu.VMEM((N, 2, D), BF16),
            pltpu.VMEM((N, 2, D), BF16),
            pltpu.VMEM((2 * N, D), F32),
            pltpu.VMEM((N, 2, 384), F32),
            pltpu.VMEM((N, 2, 384), F32),
            pltpu.VMEM((2, 3 * D + 128), F32),
            pltpu.VMEM((N, 1, 2 * D + 256), F32),
            pltpu.VMEM((N, 2, D), BF16),
            pltpu.VMEM((N, 2, 256), F32),
            pltpu.VMEM((N, 2, 256), F32),
            pltpu.VMEM((2, D + 128), F32),
            pltpu.VMEM((N, 2, D), BF16),
            pltpu.VMEM((2 * N, D), F32),
            pltpu.VMEM((N, 2, D), BF16),
            pltpu.VMEM((N, 2, D), BF16),
            pltpu.SemaphoreType.DMA((8,)),
            pltpu.SemaphoreType.DMA((10,)),
            pltpu.SemaphoreType.DMA((10,)),
        ],
        compiler_params=pltpu.CompilerParams(
            collective_id=0, has_side_effects=True, vmem_limit_bytes=40 << 20
        ),
    )(
        lengths,
        move_offset,
        pair_mask,
        keep_list,
        merge_index,
        row(merge_table),
        row(qk_scale),
        row(attn_rate),
        row(mlp_rate),
        row(up_scale),
        row(gate_scale),
        tokens,
        kv_cache,
        w_qkv,
        w_out,
        w_up,
        w_gate,
        w_down,
    )


def solution(mesh):
    return jax.shard_map(
        per_device,
        mesh=mesh,
        in_specs=(
            P(("group", "shard"), None),
            P(("group", "shard"), None, None),
            P(("group", "shard"), None),
            P(("group", "shard")),
            P(("group", "shard"), None),
            P(),
            P("shard", None),
            P("shard"),
            P(None, "shard"),
            P(None, "shard"),
            P(None, "shard"),
            P(None, "shard"),
            P("shard", None),
            P(),
            P(),
            P(),
            P("shard"),
            P("shard"),
        ),
        out_specs=(P(("group", "shard"), None), P(("group", "shard"), None, None)),
        check_vma=False,
    )
```

```python
import functools
import math

import jax
import jax.numpy as jnp
from jax import lax
from jax.experimental import pallas as pl
from jax.experimental.pallas import tpu as pltpu
from jax.sharding import PartitionSpec as P

DH = 64
WTAB = 16
N = 16
D = 1280
PARTS = 2
WIDE = 2 * D // PARTS
KEY_PARTS = PARTS // 2
HOPS = 10
HEADS_PAD = 32
EPSILON = 1e-06
NEGATIVE = -1e30
MESH = pl.DeviceIdType.MESH
F32 = jnp.float32
BF16 = jnp.bfloat16


def iota(shape, axis):
    return lax.broadcasted_iota(jnp.int32, shape, axis)


def rms_normal(vector):
    return vector * lax.rsqrt(jnp.mean(vector * vector, axis=-1, keepdims=True) + EPSILON)


def times_transposed(rows, weight):
    return lax.dot_general(rows, weight, (((1,), (1,)), ((), ())), preferred_element_type=F32)


def wait_for(ref, sem):
    pltpu.make_async_copy(ref, ref, sem).wait()


def layer_kernel(
    lengths,
    offsets,
    pair_bits,
    keep_ref,
    index_ref,
    table_ref,
    qk_ref,
    attn_rate_ref,
    mlp_rate_ref,
    up_scale_ref,
    gate_scale_ref,
    tokens_hbm,
    kv_hbm,
    w_qkv_hbm,
    w_out_hbm,
    w_up_hbm,
    w_gate_hbm,
    w_down_hbm,
    hidden_out,
    cache_out,
    kv,
    w_qkv,
    w_out,
    w_up,
    w_gate,
    w_down,
    packed,
    arrived,
    staged,
    group_rows,
    shard_rows,
    lhs,
    qkv_send,
    qkv_recv,
    qkv_flat,
    partial_wide,
    partial,
    attended_rows,
    out_send,
    out_recv,
    out_flat,
    mixed_rows,
    sum_wide,
    sum_send,
    sum_recv,
    local_sem,
    send_sem,
    recv_sem,
):
    my_group = lax.axis_index("group")
    my_shard = lax.axis_index("shard")

    def group_peer(k):
        return (lax.rem(my_group + k, N), my_shard)

    def shard_peer(k):
        return (my_group, lax.rem(my_shard + k, N))

    loads = []
    for number, (source, target) in enumerate(
        (
            (tokens_hbm, group_rows.at[0]),
            (kv_hbm, kv),
            (w_qkv_hbm, w_qkv),
            (w_out_hbm, w_out),
            (w_up_hbm, w_up),
            (w_gate_hbm, w_gate),
            (w_down_hbm, w_down),
        )
    ):
        copy = pltpu.make_async_copy(source, target, local_sem.at[number])
        copy.start()
        loads.append(copy)

    barrier = pltpu.get_barrier_semaphore()

    def greet(k, carry):
        pl.semaphore_signal(barrier, inc=1, device_id=group_peer(k), device_id_type=MESH)
        pl.semaphore_signal(barrier, inc=1, device_id=shard_peer(k), device_id_type=MESH)
        return carry

    lax.fori_loop(1, N, greet, 0)

    def push(source, target, peer, hop, stride=1):
        def one(k):
            pltpu.make_async_remote_copy(
                src_ref=source(k),
                dst_ref=target(k),
                send_sem=send_sem.at[hop],
                recv_sem=recv_sem.at[hop],
                device_id=peer(k),
                device_id_type=MESH,
            ).start()

        one(N // 2)

        def pair(step, carry):
            one(N // 2 - stride * step)
            one(N // 2 + stride * step)
            return carry

        lax.fori_loop(1, N // 2 // stride, pair, 0)

    def others(ref):
        return ref.at[pl.ds(1, N - 1)]

    def gather(rows, peer, hop):
        push(lambda k: rows.at[0], lambda k: rows.at[k], peer, hop)

    sibling = my_group + 1 - 2 * lax.rem(my_group, 2)

    def gather_group(rows, hop):
        push(lambda k: rows.at[0], lambda k: rows.at[lax.div(k, 2)], group_peer, hop, 2)

    def relay_group(rows, hop, relay_hop):
        wait_for(rows.at[pl.ds(1, N // 2 - 1)], recv_sem.at[hop])
        pltpu.make_async_remote_copy(
            src_ref=rows.at[pl.ds(0, N // 2)],
            dst_ref=rows.at[pl.ds(N // 2, N // 2)],
            send_sem=send_sem.at[relay_hop],
            recv_sem=recv_sem.at[relay_hop],
            device_id=(sibling, my_shard),
            device_id_type=MESH,
        ).start()
        wait_for(rows.at[pl.ds(N // 2, N // 2)], recv_sem.at[relay_hop])

    def slot_of(group):
        back = lax.rem(my_group - group + 2 * N, N)
        sibling_back = lax.rem(sibling - group + 2 * N, N)
        odd = lax.rem(back, 2)
        return (1 - odd) * lax.div(back, 2) + odd * (N // 2 + lax.div(sibling_back, 2))

    def give_back(source, target, hop):
        push(lambda k: source.at[k], lambda k: target.at[k], lambda k: shard_peer(N - k), hop)

    rows2 = iota((2, 128), 0)
    lane = iota((1, 128), 1)
    length2 = jnp.where(rows2 == 0, lengths[0], lengths[1])
    in_length = iota((2, 128), 1) < length2
    keeper = jnp.where((keep_ref[...] == 1) & in_length, 1.0, 0.0)
    dropper = jnp.where((keep_ref[...] == 0) & in_length, 1.0, 0.0)
    lower = jnp.where(iota((128, 128), 0) <= iota((128, 128), 1), 1.0, 0.0).astype(BF16)
    position = jnp.dot(keeper.astype(BF16), lower, preferred_element_type=F32)
    place2 = jnp.where(keeper > 0.0, position - 1.0, -1.0)
    kept = jnp.sum(keeper, axis=1, keepdims=True)
    live2 = kept + jnp.where(jnp.sum(dropper, axis=1, keepdims=True) > 0.0, 1.0, 0.0)
    table_square = jnp.broadcast_to(table_ref[...].astype(F32), (WTAB, WTAB))
    table_column = jnp.sum(
        jnp.where(iota((WTAB, WTAB), 0) == iota((WTAB, WTAB), 1), table_square, 0.0),
        axis=1,
        keepdims=True,
    )
    target_row = iota((128, 128), 0).astype(F32)
    loads[1].wait()
    for j in range(2):
        hit = iota((WTAB, 128), 0) == index_ref[j : j + 1, :]
        weights = (
            jnp.sum(jnp.where(hit, table_column, 0.0), axis=0, keepdims=True)
            * dropper[j : j + 1, :]
        )
        placing = jnp.where(target_row == place2[j : j + 1, :], 1.0, 0.0)
        summing = jnp.where(target_row == kept[j : j + 1, :], weights, 0.0)
        mixing = (placing + summing).astype(BF16)
        for part in range(PARTS):
            columns = slice(WIDE * part, WIDE * part + WIDE)
            result = jnp.dot(mixing, kv[j, :, columns], preferred_element_type=F32)
            packed[part, 8 * j : 8 * j + 8] = result.astype(BF16).reshape(8, 16, WIDE)

    loads[0].wait()
    pl.semaphore_wait(barrier, 2 * (N - 1))

    gather_group(group_rows, 0)

    def spread_cache(part):
        push(
            lambda k: packed.at[part, lax.rem(my_group + k, N)],
            lambda k: arrived[part].at[k],
            group_peer,
            HOPS + part,
        )
        arrived[part][0] = packed[part, my_group]

    for part in range(PARTS):
        spread_cache(part)

    landing_slot = lax.div(my_group, 8)
    landing_rows = pl.ds(pl.multiple_of(16 * lax.rem(my_group, 8), 16), 16)
    my_offset = offsets[0, landing_slot]
    own_chunks = []

    def deliver_cache(part):
        wait_for(others(arrived[part]), recv_sem.at[HOPS + part])
        for m in range(N):
            staged[part, m] = arrived[part][lax.rem(my_offset + N - m, N)]
        landing = cache_out.at[landing_slot, landing_rows, pl.ds(WIDE * part, WIDE)]
        push(
            lambda k: staged.at[part, k], lambda k: landing, group_peer, HOPS + PARTS + part
        )
        own_chunk = pltpu.make_async_copy(staged.at[part, 0], landing, local_sem.at[7 + part])
        own_chunk.start()
        own_chunks.append(own_chunk)

    relay_group(group_rows, 0, 8)
    offset0 = offsets[0, 0]
    offset1 = offsets[0, 1]
    first = iota((2, D), 0) == 0
    own_tokens = group_rows[0].astype(F32)
    moved_tokens = jnp.where(
        first,
        group_rows[slot_of(my_group + offset0)].astype(F32),
        group_rows[slot_of(my_group + offset1)].astype(F32),
    )
    shard_rows[0] = moved_tokens.astype(BF16)
    gather(shard_rows, shard_peer, 1)

    def stack(rows):
        for k in range(N):
            lhs[2 * k : 2 * k + 2, :] = rows[k].astype(F32)
        return lhs[...].astype(BF16)

    def shifter(width, frame):
        shift = lax.rem(width * my_shard, 128)
        return jnp.where(
            iota((width, frame), 1) == iota((width, frame), 0) + shift, 1.0, 0.0
        ).astype(BF16)

    def spread_back(rows, weight, width, frame, send, recv, flat, hop):
        columns = times_transposed(rows, weight).astype(BF16)
        framed = jnp.dot(columns, shifter(width, frame), preferred_element_type=F32)
        for k in range(N):
            send[k] = framed[2 * k : 2 * k + 2, :]
        recv[0] = framed[0:2, :]
        give_back(send, recv, hop)
        flat[...] = jnp.zeros(flat.shape, F32)
        wait_for(others(recv), recv_sem.at[hop])
        for c in range(N):
            begin = 128 * ((width * c) // 128)
            flat[:, begin : begin + frame] += recv[lax.rem(c + N - my_shard, N)]

    loads[2].wait()
    wait_for(others(shard_rows), recv_sem.at[1])
    spread_back(stack(shard_rows), w_qkv[...], 240, 384, qkv_send, qkv_recv, qkv_flat, 2)

    head_mask = lax.shift_right_logical(iota((HEADS_PAD, D), 1), 6) == iota((HEADS_PAD, D), 0)
    stat_row = iota((HEADS_PAD, 128), 0)
    stat_column = iota((HEADS_PAD, 128), 1)
    stat_lane = stat_column == stat_row
    stat_lane1 = stat_column == stat_row + HEADS_PAD
    stat_lane2 = stat_column == stat_row + 2 * HEADS_PAD
    stat_any = stat_lane | stat_lane1 | stat_lane2
    scaling = qk_ref[...][None, :]
    score_scale = float(DH) ** 0.5

    def heads(row):
        masked = jnp.where(head_mask, jnp.broadcast_to(row, (HEADS_PAD, D)), 0.0)
        squares = jnp.sum(masked * masked, axis=1, keepdims=True)
        return (masked * lax.rsqrt(squares + EPSILON) * scaling).astype(BF16)

    home = lax.rem(my_group + offset1, N)
    partner_here = jnp.bitwise_xor(home, pair_bits[0, 0])
    for j in range(2):
        queries = heads(qkv_flat[j : j + 1, 0:D])
        new_keys = heads(qkv_flat[j : j + 1, D : 2 * D])
        new_values = qkv_flat[j : j + 1, 2 * D : 3 * D]
        scores = sum(
            times_transposed(
                queries[:, WIDE * part : WIDE * part + WIDE],
                packed[part, 8 * j : 8 * j + 8].reshape(128, WIDE),
            )
            for part in range(KEY_PARTS)
        )
        scores = score_scale * scores
        fresh = score_scale * jnp.sum(
            queries.astype(F32) * new_keys.astype(F32), axis=1, keepdims=True
        )
        if j == 1:
            counted = jnp.full((HEADS_PAD, 1), home, jnp.int32) < partner_here
        else:
            counted = jnp.full((HEADS_PAD, 1), True)
        valid = jnp.broadcast_to(lane.astype(F32) < live2[j : j + 1, :], (HEADS_PAD, 128))
        highest = jnp.maximum(
            jnp.max(jnp.where(valid, scores, NEGATIVE), axis=1, keepdims=True),
            jnp.where(counted, fresh, NEGATIVE),
        )
        soft = jnp.where(valid, jnp.exp(jnp.where(valid, scores - highest, 0.0)), 0.0)
        fresh_weight = jnp.where(counted, jnp.exp(fresh - highest), 0.0)
        weight_sum = jnp.sum(soft, axis=1, keepdims=True) + fresh_weight
        fresh_low = fresh_weight.astype(BF16).astype(F32)
        for part in range(KEY_PARTS):
            columns = slice(WIDE * part, WIDE * part + WIDE)
            values = packed[KEY_PARTS + part, 8 * j : 8 * j + 8].reshape(128, WIDE)
            weighted = jnp.dot(soft.astype(BF16), values, preferred_element_type=F32)
            weighted = weighted + fresh_low * new_values[:, columns]
            partial_wide[j : j + 1, columns] = jnp.sum(
                jnp.where(head_mask[:, columns], weighted / weight_sum, 0.0),
                axis=0,
                keepdims=True,
            )
    total = highest + jnp.log(weight_sum)
    piece0 = total.astype(BF16).astype(F32)
    piece1 = (total - piece0).astype(BF16).astype(F32)
    piece2 = total - piece0 - piece1
    pieces = jnp.where(stat_lane, piece0, 0.0)
    pieces = pieces + jnp.where(stat_lane1, piece1, 0.0)
    pieces = pieces + jnp.where(stat_lane2, piece2, 0.0)
    partial_wide[0:1, D : D + 128] = jnp.zeros((1, 128), F32)
    partial_wide[1:2, D : D + 128] = jnp.sum(pieces, axis=0, keepdims=True)
    partial[0] = partial_wide[...].astype(BF16)

    gather_group(partial, 3)

    deliver_cache(0)

    relay_group(partial, 3, 9)
    partner = jnp.bitwise_xor(my_group, pair_bits[0, 0])
    mine = partial[slot_of(my_group - offset1)].astype(F32)[1:2, :]
    other = partial[slot_of(partner - offset1)].astype(F32)[1:2, :]

    def total_of(row):
        pieces = jnp.broadcast_to(row[:, D : D + 128], (HEADS_PAD, 128))
        return jnp.sum(jnp.where(stat_any, pieces, 0.0), axis=1, keepdims=True)

    def by_column(column):
        return jnp.sum(jnp.where(head_mask, column, 0.0), axis=0, keepdims=True)

    my_total = total_of(mine)
    other_total = total_of(other)
    merged = jnp.maximum(my_total, other_total)
    my_factor = jnp.exp(my_total - merged)
    other_factor = jnp.exp(other_total - merged)
    both = my_factor + other_factor
    long_row = mine[:, 0:D] * by_column(my_factor / both) + other[:, 0:D] * by_column(
        other_factor / both
    )
    short_row = partial[slot_of(my_group - offset0)].astype(F32)[0:1, 0:D]
    attended = jnp.where(
        first, jnp.broadcast_to(short_row, (2, D)), jnp.broadcast_to(long_row, (2, D))
    )
    attended_rows[0] = attended.astype(BF16)
    gather(attended_rows, shard_peer, 4)
    for part in range(1, PARTS):
        deliver_cache(part)

    loads[3].wait()
    wait_for(others(attended_rows), recv_sem.at[4])
    spread_back(stack(attended_rows), w_out[...], 80, 256, out_send, out_recv, out_flat, 5)
    attention_out = out_flat[:, 0:D]
    mixed = rms_normal(
        own_tokens + attn_rate_ref[...][None, :] * (rms_normal(attention_out) - own_tokens)
    )
    mixed_rows[0] = mixed.astype(BF16)
    gather(mixed_rows, shard_peer, 6)

    loads[4].wait()
    loads[5].wait()
    loads[6].wait()
    wait_for(others(mixed_rows), recv_sem.at[6])
    rows = stack(mixed_rows)
    up = times_transposed(rows, w_up[...]) * up_scale_ref[...][None, :]
    gate = times_transposed(rows, w_gate[...]) * (
        gate_scale_ref[...][None, :] * float(D) ** 0.5
    )
    inner = (up * (gate / (1.0 + jnp.exp(-gate)))).astype(BF16)
    sum_wide[...] = jnp.dot(inner, w_down[...], preferred_element_type=F32)
    for k in range(N):
        sum_send[k] = sum_wide[2 * k : 2 * k + 2, :].astype(BF16)
    sum_recv[0] = sum_send[0]
    give_back(sum_send, sum_recv, 7)
    wait_for(others(sum_recv), recv_sem.at[7])
    mlp_out = sum_recv[0].astype(F32)
    for k in range(1, N):
        mlp_out = mlp_out + sum_recv[k].astype(F32)
    hidden_out[...] = rms_normal(
        mixed + mlp_rate_ref[...][None, :] * (rms_normal(mlp_out) - mixed)
    ).astype(BF16)

    for part in range(PARTS):
        wait_for(others(staged.at[part]), recv_sem.at[HOPS + PARTS + part])
        own_chunks[part].wait()
    half = pl.ds(N // 2, N // 2)
    most = pl.ds(1, N // 2 - 1)
    sent = (
        [
            group_rows.at[most],
            others(shard_rows),
            others(qkv_recv),
            partial.at[most],
            others(attended_rows),
            others(out_recv),
            others(mixed_rows),
            others(sum_recv),
            group_rows.at[half],
            partial.at[half],
        ]
        + [others(arrived[part]) for part in range(PARTS)]
        + [others(staged.at[part]) for part in range(PARTS)]
    )
    for hop, ref in enumerate(sent):
        wait_for(ref, send_sem.at[hop])


def per_device(
    tokens,
    kv_cache,
    keep_list,
    lengths,
    merge_index,
    merge_table,
    move_offset,
    pair_mask,
    w_qkv,
    w_out,
    w_up,
    w_gate,
    w_down,
    qk_scale,
    attn_rate,
    mlp_rate,
    up_scale,
    gate_scale,
):
    smem = pl.BlockSpec(memory_space=pltpu.SMEM)
    vmem = pl.BlockSpec(memory_space=pltpu.VMEM)
    hbm = pl.BlockSpec(memory_space=pltpu.HBM)

    return pl.pallas_call(
        layer_kernel,
        out_shape=(
            pltpu.VMEM((2, D), BF16),
            pltpu.VMEM((2, 128, 2 * D), BF16),
        ),
        in_specs=[smem] * 3 + [vmem] * 8 + [hbm] * 7,
        out_specs=(vmem, pl.BlockSpec(memory_space=pl.ANY)),
        scratch_shapes=[
            pltpu.VMEM((2, 128, 2 * D), BF16),
            pltpu.VMEM((240, D), BF16),
            pltpu.VMEM((80, D), BF16),
            pltpu.VMEM((320, D), BF16),
            pltpu.VMEM((320, D), BF16),
            pltpu.VMEM((320, D), BF16),
            pltpu.VMEM((PARTS, N, 16, WIDE), BF16),
            [pltpu.VMEM((N, 16, WIDE), BF16)] * PARTS,
            pltpu.VMEM((PARTS, N, 16, WIDE), BF16),
            pltpu.VMEM((N, 2, D), BF16),
            pltpu.VMEM((N, 2, D), BF16),
            pltpu.VMEM((2 * N, D), F32),
            pltpu.VMEM((N, 2, 384), F32),
            pltpu.VMEM((N, 2, 384), F32),
            pltpu.VMEM((2, 3 * D + 128), F32),
            pltpu.VMEM((2, D + 128), F32),
            pltpu.VMEM((N, 2, D + 128), BF16),
            pltpu.VMEM((N, 2, D), BF16),
            pltpu.VMEM((N, 2, 256), F32),
            pltpu.VMEM((N, 2, 256), F32),
            pltpu.VMEM((2, D + 128), F32),
            pltpu.VMEM((N, 2, D), BF16),
            pltpu.VMEM((2 * N, D), F32),
            pltpu.VMEM((N, 2, D), BF16),
            pltpu.VMEM((N, 2, D), BF16),
            pltpu.SemaphoreType.DMA((7 + PARTS,)),
            pltpu.SemaphoreType.DMA((HOPS + 2 * PARTS,)),
            pltpu.SemaphoreType.DMA((HOPS + 2 * PARTS,)),
        ],
        compiler_params=pltpu.CompilerParams(
            collective_id=0, has_side_effects=True, vmem_limit_bytes=60 << 20
        ),
    )(
        lengths,
        move_offset,
        pair_mask[None, :],
        keep_list,
        merge_index,
        merge_table[None, :],
        qk_scale,
        attn_rate,
        mlp_rate,
        up_scale,
        gate_scale,
        tokens,
        kv_cache,
        w_qkv.T,
        w_out.T,
        w_up.T,
        w_gate.T,
        w_down,
    )


def solution(mesh):
    return jax.shard_map(
        per_device,
        mesh=mesh,
        in_specs=(
            P(("group", "shard"), None),
            P(("group", "shard"), None, None),
            P(("group", "shard"), None),
            P(("group", "shard")),
            P(("group", "shard"), None),
            P(),
            P("shard", None),
            P("shard"),
            P(None, "shard"),
            P(None, "shard"),
            P(None, "shard"),
            P(None, "shard"),
            P("shard", None),
            P(),
            P(),
            P(),
            P("shard"),
            P("shard"),
        ),
        out_specs=(P(("group", "shard"), None), P(("group", "shard"), None, None)),
        check_vma=False,
    )
```

```python
import functools
import math

import jax
import jax.numpy as jnp
from jax import lax
from jax.experimental import pallas as pl
from jax.experimental.pallas import tpu as pltpu
from jax.sharding import PartitionSpec as P

DH = 64
WTAB = 16
N = 16
D = 1280
PARTS = 2
WIDE = 2 * D // PARTS
KEY_PARTS = PARTS // 2
HOPS = 10
HEADS_PAD = 32
EPSILON = 1e-06
NEGATIVE = -1e30
MESH = pl.DeviceIdType.MESH
F32 = jnp.float32
BF16 = jnp.bfloat16


def iota(shape, axis):
    return lax.broadcasted_iota(jnp.int32, shape, axis)


def rms_normal(vector):
    return vector * lax.rsqrt(jnp.mean(vector * vector, axis=-1, keepdims=True) + EPSILON)


def times_transposed(rows, weight):
    return lax.dot_general(rows, weight, (((1,), (1,)), ((), ())), preferred_element_type=F32)


def wait_for(ref, sem):
    pltpu.make_async_copy(ref, ref, sem).wait()


def layer_kernel(
    lengths_hbm,
    offsets_hbm,
    pair_bits_hbm,
    keep_hbm,
    index_hbm,
    table_hbm,
    qk_hbm,
    attn_rate_hbm,
    mlp_rate_hbm,
    up_scale_hbm,
    gate_scale_hbm,
    tokens_hbm,
    kv_hbm,
    w_qkv_hbm,
    w_out_hbm,
    w_up_hbm,
    w_gate_hbm,
    w_down_hbm,
    hidden_out,
    cache_out,
    lengths,
    offsets,
    pair_bits,
    keep_ref,
    index_ref,
    table_ref,
    qk_ref,
    attn_rate_ref,
    mlp_rate_ref,
    up_scale_ref,
    gate_scale_ref,
    kv,
    w_qkv,
    w_out,
    w_up,
    w_gate,
    w_down,
    packed,
    arrived,
    staged,
    group_rows,
    shard_rows,
    lhs,
    qkv_send,
    qkv_recv,
    qkv_flat,
    partial_wide,
    partial,
    attended_rows,
    out_send,
    out_recv,
    out_flat,
    mixed_rows,
    sum_wide,
    sum_send,
    sum_recv,
    local_sem,
    send_sem,
    recv_sem,
):
    my_group = lax.axis_index("group")
    my_shard = lax.axis_index("shard")

    def group_peer(k):
        return (lax.rem(my_group + k, N), my_shard)

    def shard_peer(k):
        return (my_group, lax.rem(my_shard + k, N))

    barrier = pltpu.get_barrier_semaphore()

    def greet(k, carry):
        pl.semaphore_signal(barrier, inc=1, device_id=group_peer(k), device_id_type=MESH)
        pl.semaphore_signal(barrier, inc=1, device_id=shard_peer(k), device_id_type=MESH)
        return carry

    lax.fori_loop(1, N, greet, 0)

    loads = []
    for number, (source, target) in enumerate(
        (
            (tokens_hbm, group_rows.at[0]),
            (kv_hbm, kv),
            (w_qkv_hbm, w_qkv),
            (w_out_hbm, w_out),
            (w_up_hbm, w_up),
            (w_gate_hbm, w_gate),
            (w_down_hbm, w_down),
            (lengths_hbm, lengths),
            (keep_hbm, keep_ref),
            (index_hbm, index_ref),
            (table_hbm, table_ref),
            (offsets_hbm, offsets),
            (pair_bits_hbm, pair_bits),
            (qk_hbm, qk_ref),
            (attn_rate_hbm, attn_rate_ref),
            (mlp_rate_hbm, mlp_rate_ref),
            (up_scale_hbm, up_scale_ref),
            (gate_scale_hbm, gate_scale_ref),
        )
    ):
        copy = pltpu.make_async_copy(source, target, local_sem.at[number])
        copy.start()
        loads.append(copy)

    def push(source, target, peer, hop, stride=1):
        def one(k):
            pltpu.make_async_remote_copy(
                src_ref=source(k),
                dst_ref=target(k),
                send_sem=send_sem.at[hop],
                recv_sem=recv_sem.at[hop],
                device_id=peer(k),
                device_id_type=MESH,
            ).start()

        one(N // 2)

        def pair(step, carry):
            one(N // 2 - stride * step)
            one(N // 2 + stride * step)
            return carry

        lax.fori_loop(1, N // 2 // stride, pair, 0)

    def others(ref):
        return ref.at[pl.ds(1, N - 1)]

    def gather(rows, peer, hop):
        push(lambda k: rows.at[0], lambda k: rows.at[k], peer, hop)

    sibling = my_group + 1 - 2 * lax.rem(my_group, 2)

    def gather_group(rows, hop):
        push(lambda k: rows.at[0], lambda k: rows.at[lax.div(k, 2)], group_peer, hop, 2)

    def relay_group(rows, hop, relay_hop):
        wait_for(rows.at[pl.ds(1, N // 2 - 1)], recv_sem.at[hop])
        pltpu.make_async_remote_copy(
            src_ref=rows.at[pl.ds(0, N // 2)],
            dst_ref=rows.at[pl.ds(N // 2, N // 2)],
            send_sem=send_sem.at[relay_hop],
            recv_sem=recv_sem.at[relay_hop],
            device_id=(sibling, my_shard),
            device_id_type=MESH,
        ).start()
        wait_for(rows.at[pl.ds(N // 2, N // 2)], recv_sem.at[relay_hop])

    def slot_of(group):
        back = lax.rem(my_group - group + 2 * N, N)
        sibling_back = lax.rem(sibling - group + 2 * N, N)
        odd = lax.rem(back, 2)
        return (1 - odd) * lax.div(back, 2) + odd * (N // 2 + lax.div(sibling_back, 2))

    def give_back(source, target, hop):
        push(lambda k: source.at[k], lambda k: target.at[k], lambda k: shard_peer(N - k), hop)

    for number in range(7, 11):
        loads[number].wait()
    rows2 = iota((2, 128), 0)
    lane = iota((1, 128), 1)
    length2 = jnp.where(rows2 == 0, lengths[0], lengths[1])
    in_length = iota((2, 128), 1) < length2
    keeper = jnp.where((keep_ref[...] == 1) & in_length, 1.0, 0.0)
    dropper = jnp.where((keep_ref[...] == 0) & in_length, 1.0, 0.0)
    lower = jnp.where(iota((128, 128), 0) <= iota((128, 128), 1), 1.0, 0.0).astype(BF16)
    position = jnp.dot(keeper.astype(BF16), lower, preferred_element_type=F32)
    place2 = jnp.where(keeper > 0.0, position - 1.0, -1.0)
    kept = jnp.sum(keeper, axis=1, keepdims=True)
    live2 = kept + jnp.where(jnp.sum(dropper, axis=1, keepdims=True) > 0.0, 1.0, 0.0)
    table_square = jnp.broadcast_to(table_ref[...].astype(F32), (WTAB, WTAB))
    table_column = jnp.sum(
        jnp.where(iota((WTAB, WTAB), 0) == iota((WTAB, WTAB), 1), table_square, 0.0),
        axis=1,
        keepdims=True,
    )
    target_row = iota((128, 128), 0).astype(F32)
    mixings = []
    for j in range(2):
        hit = iota((WTAB, 128), 0) == index_ref[j : j + 1, :]
        weights = (
            jnp.sum(jnp.where(hit, table_column, 0.0), axis=0, keepdims=True)
            * dropper[j : j + 1, :]
        )
        placing = jnp.where(target_row == place2[j : j + 1, :], 1.0, 0.0)
        summing = jnp.where(target_row == kept[j : j + 1, :], weights, 0.0)
        mixings.append((placing + summing).astype(BF16))
    loads[1].wait()

    def compact(part):
        columns = slice(WIDE * part, WIDE * part + WIDE)
        for j in range(2):
            result = jnp.dot(mixings[j], kv[j, :, columns], preferred_element_type=F32)
            packed[part, 8 * j : 8 * j + 8] = result.astype(BF16).reshape(8, 16, WIDE)

    compact(0)

    loads[0].wait()
    pl.semaphore_wait(barrier, 2 * (N - 1))

    gather_group(group_rows, 0)

    def spread_cache(part):
        push(
            lambda k: packed.at[part, lax.rem(my_group + k, N)],
            lambda k: arrived[part].at[k],
            group_peer,
            HOPS + part,
        )
        arrived[part][0] = packed[part, my_group]

    spread_cache(0)
    for part in range(1, PARTS):
        compact(part)
        spread_cache(part)
    for number in range(11, 18):
        loads[number].wait()

    landing_slot = lax.div(my_group, 8)
    landing_rows = pl.ds(pl.multiple_of(16 * lax.rem(my_group, 8), 16), 16)
    my_offset = offsets[0, landing_slot]
    own_chunks = []

    def deliver_cache(part):
        wait_for(others(arrived[part]), recv_sem.at[HOPS + part])
        for m in range(N):
            staged[part, m] = arrived[part][lax.rem(my_offset + N - m, N)]
        landing = cache_out.at[landing_slot, landing_rows, pl.ds(WIDE * part, WIDE)]
        push(
            lambda k: staged.at[part, k], lambda k: landing, group_peer, HOPS + PARTS + part
        )
        own_chunk = pltpu.make_async_copy(staged.at[part, 0], landing, local_sem.at[18 + part])
        own_chunk.start()
        own_chunks.append(own_chunk)

    relay_group(group_rows, 0, 8)
    offset0 = offsets[0, 0]
    offset1 = offsets[0, 1]
    first = iota((2, D), 0) == 0
    own_tokens = group_rows[0].astype(F32)
    moved_tokens = jnp.where(
        first,
        group_rows[slot_of(my_group + offset0)].astype(F32),
        group_rows[slot_of(my_group + offset1)].astype(F32),
    )
    shard_rows[0] = moved_tokens.astype(BF16)
    gather(shard_rows, shard_peer, 1)

    def stack(rows):
        for k in range(N):
            lhs[2 * k : 2 * k + 2, :] = rows[k].astype(F32)
        return lhs[...].astype(BF16)

    def shifter(width, frame):
        shift = lax.rem(width * my_shard, 128)
        return jnp.where(
            iota((width, frame), 1) == iota((width, frame), 0) + shift, 1.0, 0.0
        ).astype(BF16)

    def spread_back(rows, weight, width, frame, send, recv, flat, hop):
        columns = times_transposed(rows, weight).astype(BF16)
        framed = jnp.dot(columns, shifter(width, frame), preferred_element_type=F32)
        for k in range(N):
            send[k] = framed[2 * k : 2 * k + 2, :]
        recv[0] = framed[0:2, :]
        give_back(send, recv, hop)
        flat[...] = jnp.zeros(flat.shape, F32)
        wait_for(others(recv), recv_sem.at[hop])
        for c in range(N):
            begin = 128 * ((width * c) // 128)
            flat[:, begin : begin + frame] += recv[lax.rem(c + N - my_shard, N)]

    loads[2].wait()
    wait_for(others(shard_rows), recv_sem.at[1])
    spread_back(stack(shard_rows), w_qkv[...], 240, 384, qkv_send, qkv_recv, qkv_flat, 2)

    head_mask = lax.shift_right_logical(iota((HEADS_PAD, D), 1), 6) == iota((HEADS_PAD, D), 0)
    stat_row = iota((HEADS_PAD, 128), 0)
    stat_column = iota((HEADS_PAD, 128), 1)
    stat_lane = stat_column == stat_row
    stat_lane1 = stat_column == stat_row + HEADS_PAD
    stat_lane2 = stat_column == stat_row + 2 * HEADS_PAD
    stat_any = stat_lane | stat_lane1 | stat_lane2
    scaling = qk_ref[...][None, :]
    score_scale = float(DH) ** 0.5

    def heads(row):
        masked = jnp.where(head_mask, jnp.broadcast_to(row, (HEADS_PAD, D)), 0.0)
        squares = jnp.sum(masked * masked, axis=1, keepdims=True)
        return (masked * lax.rsqrt(squares + EPSILON) * scaling).astype(BF16)

    home = lax.rem(my_group + offset1, N)
    partner_here = jnp.bitwise_xor(home, pair_bits[0, 0])
    for j in range(2):
        queries = heads(qkv_flat[j : j + 1, 0:D])
        new_keys = heads(qkv_flat[j : j + 1, D : 2 * D])
        new_values = qkv_flat[j : j + 1, 2 * D : 3 * D]
        scores = sum(
            times_transposed(
                queries[:, WIDE * part : WIDE * part + WIDE],
                packed[part, 8 * j : 8 * j + 8].reshape(128, WIDE),
            )
            for part in range(KEY_PARTS)
        )
        scores = score_scale * scores
        fresh = score_scale * jnp.sum(
            queries.astype(F32) * new_keys.astype(F32), axis=1, keepdims=True
        )
        if j == 1:
            counted = jnp.full((HEADS_PAD, 1), home, jnp.int32) < partner_here
        else:
            counted = jnp.full((HEADS_PAD, 1), True)
        valid = jnp.broadcast_to(lane.astype(F32) < live2[j : j + 1, :], (HEADS_PAD, 128))
        highest = jnp.maximum(
            jnp.max(jnp.where(valid, scores, NEGATIVE), axis=1, keepdims=True),
            jnp.where(counted, fresh, NEGATIVE),
        )
        soft = jnp.where(valid, jnp.exp(jnp.where(valid, scores - highest, 0.0)), 0.0)
        fresh_weight = jnp.where(counted, jnp.exp(fresh - highest), 0.0)
        weight_sum = jnp.sum(soft, axis=1, keepdims=True) + fresh_weight
        fresh_low = fresh_weight.astype(BF16).astype(F32)
        for part in range(KEY_PARTS):
            columns = slice(WIDE * part, WIDE * part + WIDE)
            values = packed[KEY_PARTS + part, 8 * j : 8 * j + 8].reshape(128, WIDE)
            weighted = jnp.dot(soft.astype(BF16), values, preferred_element_type=F32)
            weighted = weighted + fresh_low * new_values[:, columns]
            partial_wide[j : j + 1, columns] = jnp.sum(
                jnp.where(head_mask[:, columns], weighted / weight_sum, 0.0),
                axis=0,
                keepdims=True,
            )
    total = highest + jnp.log(weight_sum)
    piece0 = total.astype(BF16).astype(F32)
    piece1 = (total - piece0).astype(BF16).astype(F32)
    piece2 = total - piece0 - piece1
    pieces = jnp.where(stat_lane, piece0, 0.0)
    pieces = pieces + jnp.where(stat_lane1, piece1, 0.0)
    pieces = pieces + jnp.where(stat_lane2, piece2, 0.0)
    partial_wide[0:1, D : D + 128] = jnp.zeros((1, 128), F32)
    partial_wide[1:2, D : D + 128] = jnp.sum(pieces, axis=0, keepdims=True)
    partial[0] = partial_wide[...].astype(BF16)

    gather_group(partial, 3)

    deliver_cache(0)

    relay_group(partial, 3, 9)
    partner = jnp.bitwise_xor(my_group, pair_bits[0, 0])
    mine = partial[slot_of(my_group - offset1)].astype(F32)[1:2, :]
    other = partial[slot_of(partner - offset1)].astype(F32)[1:2, :]

    def total_of(row):
        pieces = jnp.broadcast_to(row[:, D : D + 128], (HEADS_PAD, 128))
        return jnp.sum(jnp.where(stat_any, pieces, 0.0), axis=1, keepdims=True)

    def by_column(column):
        return jnp.sum(jnp.where(head_mask, column, 0.0), axis=0, keepdims=True)

    my_total = total_of(mine)
    other_total = total_of(other)
    merged = jnp.maximum(my_total, other_total)
    my_factor = jnp.exp(my_total - merged)
    other_factor = jnp.exp(other_total - merged)
    both = my_factor + other_factor
    long_row = mine[:, 0:D] * by_column(my_factor / both) + other[:, 0:D] * by_column(
        other_factor / both
    )
    short_row = partial[slot_of(my_group - offset0)].astype(F32)[0:1, 0:D]
    attended = jnp.where(
        first, jnp.broadcast_to(short_row, (2, D)), jnp.broadcast_to(long_row, (2, D))
    )
    attended_rows[0] = attended.astype(BF16)
    gather(attended_rows, shard_peer, 4)
    for part in range(1, PARTS):
        deliver_cache(part)

    loads[3].wait()
    wait_for(others(attended_rows), recv_sem.at[4])
    spread_back(stack(attended_rows), w_out[...], 80, 256, out_send, out_recv, out_flat, 5)
    attention_out = out_flat[:, 0:D]
    mixed = rms_normal(
        own_tokens + attn_rate_ref[...][None, :] * (rms_normal(attention_out) - own_tokens)
    )
    mixed_rows[0] = mixed.astype(BF16)
    gather(mixed_rows, shard_peer, 6)

    loads[4].wait()
    loads[5].wait()
    loads[6].wait()
    wait_for(others(mixed_rows), recv_sem.at[6])
    rows = stack(mixed_rows)
    up = times_transposed(rows, w_up[...]) * up_scale_ref[...][None, :]
    gate = times_transposed(rows, w_gate[...]) * (
        gate_scale_ref[...][None, :] * float(D) ** 0.5
    )
    inner = (up * (gate / (1.0 + jnp.exp(-gate)))).astype(BF16)
    sum_wide[...] = jnp.dot(inner, w_down[...], preferred_element_type=F32)
    for k in range(N):
        sum_send[k] = sum_wide[2 * k : 2 * k + 2, :].astype(BF16)
    sum_recv[0] = sum_send[0]
    give_back(sum_send, sum_recv, 7)
    wait_for(others(sum_recv), recv_sem.at[7])
    mlp_out = sum_recv[0].astype(F32)
    for k in range(1, N):
        mlp_out = mlp_out + sum_recv[k].astype(F32)
    hidden_out[...] = rms_normal(
        mixed + mlp_rate_ref[...][None, :] * (rms_normal(mlp_out) - mixed)
    ).astype(BF16)

    for part in range(PARTS):
        wait_for(others(staged.at[part]), recv_sem.at[HOPS + PARTS + part])
        own_chunks[part].wait()
    half = pl.ds(N // 2, N // 2)
    most = pl.ds(1, N // 2 - 1)
    sent = (
        [
            group_rows.at[most],
            others(shard_rows),
            others(qkv_recv),
            partial.at[most],
            others(attended_rows),
            others(out_recv),
            others(mixed_rows),
            others(sum_recv),
            group_rows.at[half],
            partial.at[half],
        ]
        + [others(arrived[part]) for part in range(PARTS)]
        + [others(staged.at[part]) for part in range(PARTS)]
    )
    for hop, ref in enumerate(sent):
        wait_for(ref, send_sem.at[hop])


def finish_kernel(hidden, cache, hidden_out, cache_out, sems):
    copies = [pltpu.make_async_copy(hidden, hidden_out, sems.at[0])]
    for number in range(8):
        part = (number // 4, pl.ds(32 * (number % 4), 32))
        copies.append(
            pltpu.make_async_copy(cache.at[part], cache_out.at[part], sems.at[1 + number])
        )
    for copy in copies:
        copy.start()
    for copy in copies:
        copy.wait()


def per_device(
    tokens,
    kv_cache,
    keep_list,
    lengths,
    merge_index,
    merge_table,
    move_offset,
    pair_mask,
    w_qkv,
    w_out,
    w_up,
    w_gate,
    w_down,
    qk_scale,
    attn_rate,
    mlp_rate,
    up_scale,
    gate_scale,
):
    vmem = pl.BlockSpec(memory_space=pltpu.VMEM)
    hbm = pl.BlockSpec(memory_space=pltpu.HBM)

    hidden, cache = pl.pallas_call(
        layer_kernel,
        out_shape=(
            pltpu.VMEM((2, D), BF16),
            pltpu.VMEM((2, 128, 2 * D), BF16),
        ),
        in_specs=[hbm] * 18,
        out_specs=(vmem, pl.BlockSpec(memory_space=pl.ANY)),
        scratch_shapes=[
            pltpu.SMEM((2,), jnp.int32),
            pltpu.SMEM((1, 2), jnp.int32),
            pltpu.SMEM((1, 1), jnp.int32),
            pltpu.VMEM((2, 128), jnp.int32),
            pltpu.VMEM((2, 128), jnp.int32),
            pltpu.VMEM((1, WTAB), BF16),
            pltpu.VMEM((D,), F32),
            pltpu.VMEM((D,), F32),
            pltpu.VMEM((D,), F32),
            pltpu.VMEM((320,), F32),
            pltpu.VMEM((320,), F32),
            pltpu.VMEM((2, 128, 2 * D), BF16),
            pltpu.VMEM((240, D), BF16),
            pltpu.VMEM((80, D), BF16),
            pltpu.VMEM((320, D), BF16),
            pltpu.VMEM((320, D), BF16),
            pltpu.VMEM((320, D), BF16),
            pltpu.VMEM((PARTS, N, 16, WIDE), BF16),
            [pltpu.VMEM((N, 16, WIDE), BF16)] * PARTS,
            pltpu.VMEM((PARTS, N, 16, WIDE), BF16),
            pltpu.VMEM((N, 2, D), BF16),
            pltpu.VMEM((N, 2, D), BF16),
            pltpu.VMEM((2 * N, D), F32),
            pltpu.VMEM((N, 2, 384), F32),
            pltpu.VMEM((N, 2, 384), F32),
            pltpu.VMEM((2, 3 * D + 128), F32),
            pltpu.VMEM((2, D + 128), F32),
            pltpu.VMEM((N, 2, D + 128), BF16),
            pltpu.VMEM((N, 2, D), BF16),
            pltpu.VMEM((N, 2, 256), F32),
            pltpu.VMEM((N, 2, 256), F32),
            pltpu.VMEM((2, D + 128), F32),
            pltpu.VMEM((N, 2, D), BF16),
            pltpu.VMEM((2 * N, D), F32),
            pltpu.VMEM((N, 2, D), BF16),
            pltpu.VMEM((N, 2, D), BF16),
            pltpu.SemaphoreType.DMA((18 + PARTS,)),
            pltpu.SemaphoreType.DMA((HOPS + 2 * PARTS,)),
            pltpu.SemaphoreType.DMA((HOPS + 2 * PARTS,)),
        ],
        compiler_params=pltpu.CompilerParams(
            collective_id=0, has_side_effects=True, vmem_limit_bytes=60 << 20
        ),
    )(
        lengths,
        move_offset,
        pair_mask[None, :],
        keep_list,
        merge_index,
        merge_table[None, :],
        qk_scale,
        attn_rate,
        mlp_rate,
        up_scale,
        gate_scale,
        tokens,
        kv_cache,
        w_qkv.T,
        w_out.T,
        w_up.T,
        w_gate.T,
        w_down,
    )
    return pl.pallas_call(
        finish_kernel,
        out_shape=(
            pltpu.HBM((2, D), BF16),
            pltpu.HBM((2, 128, 2 * D), BF16),
        ),
        in_specs=[pl.BlockSpec(memory_space=pl.ANY)] * 2,
        out_specs=(pl.BlockSpec(memory_space=pl.ANY),) * 2,
        scratch_shapes=[pltpu.SemaphoreType.DMA((9,))],
    )(
        pltpu.with_memory_space_constraint(hidden, pltpu.VMEM),
        pltpu.with_memory_space_constraint(cache, pltpu.VMEM),
    )


def solution(mesh):
    return jax.shard_map(
        per_device,
        mesh=mesh,
        in_specs=(
            P(("group", "shard"), None),
            P(("group", "shard"), None, None),
            P(("group", "shard"), None),
            P(("group", "shard")),
            P(("group", "shard"), None),
            P(),
            P("shard", None),
            P("shard"),
            P(None, "shard"),
            P(None, "shard"),
            P(None, "shard"),
            P(None, "shard"),
            P("shard", None),
            P(),
            P(),
            P(),
            P("shard"),
            P("shard"),
        ),
        out_specs=(P(("group", "shard"), None), P(("group", "shard"), None, None)),
        check_vma=False,
    )
```

```python
import functools
import math

import jax
import jax.numpy as jnp
from jax import lax
from jax.experimental import pallas as pl
from jax.experimental.pallas import tpu as pltpu
from jax.sharding import PartitionSpec as P

DH = 64
WTAB = 16
N = 16
D = 1280
PARTS = 2
WIDE = 2 * D // PARTS
KEY_PARTS = PARTS // 2
HOPS = 10
HEADS_PAD = 32
EPSILON = 1e-06
NEGATIVE = -1e30
MESH = pl.DeviceIdType.MESH
F32 = jnp.float32
BF16 = jnp.bfloat16


def iota(shape, axis):
    return lax.broadcasted_iota(jnp.int32, shape, axis)


def rms_normal(vector):
    return vector * lax.rsqrt(jnp.mean(vector * vector, axis=-1, keepdims=True) + EPSILON)


def times_transposed(rows, weight):
    return lax.dot_general(rows, weight, (((1,), (1,)), ((), ())), preferred_element_type=F32)


def wait_for(ref, sem):
    pltpu.make_async_copy(ref, ref, sem).wait()


def layer_kernel(
    lengths_hbm,
    offsets_hbm,
    pair_bits_hbm,
    keep_hbm,
    index_hbm,
    table_hbm,
    qk_hbm,
    attn_rate_hbm,
    mlp_rate_hbm,
    up_scale_hbm,
    gate_scale_hbm,
    tokens_hbm,
    kv_hbm,
    w_qkv_hbm,
    w_out_hbm,
    w_up_hbm,
    w_gate_hbm,
    w_down_hbm,
    hidden_out,
    cache_out,
    lengths,
    offsets,
    pair_bits,
    keep_ref,
    index_ref,
    table_ref,
    qk_ref,
    attn_rate_ref,
    mlp_rate_ref,
    up_scale_ref,
    gate_scale_ref,
    kv,
    w_qkv,
    w_out,
    w_up,
    w_gate,
    w_down,
    packed,
    arrived,
    staged,
    group_rows,
    shard_rows,
    lhs,
    qkv_send,
    qkv_recv,
    qkv_flat,
    partial_wide,
    partial,
    attended_rows,
    out_send,
    out_recv,
    out_flat,
    mixed_rows,
    sum_wide,
    sum_send,
    sum_recv,
    local_sem,
    send_sem,
    recv_sem,
):
    my_group = lax.axis_index("group")
    my_shard = lax.axis_index("shard")

    def group_peer(k):
        return (lax.rem(my_group + k, N), my_shard)

    def shard_peer(k):
        return (my_group, lax.rem(my_shard + k, N))

    barrier = pltpu.get_barrier_semaphore()

    def greet(k, carry):
        pl.semaphore_signal(barrier, inc=1, device_id=group_peer(k), device_id_type=MESH)
        pl.semaphore_signal(barrier, inc=1, device_id=shard_peer(k), device_id_type=MESH)
        return carry

    lax.fori_loop(1, N, greet, 0)

    loads = []
    for number, (source, target) in enumerate(
        (
            (tokens_hbm, group_rows.at[0]),
            (kv_hbm, kv),
            (w_qkv_hbm, w_qkv),
            (w_out_hbm, w_out),
            (w_up_hbm, w_up),
            (w_gate_hbm, w_gate),
            (w_down_hbm, w_down),
            (lengths_hbm, lengths),
            (keep_hbm, keep_ref),
            (index_hbm, index_ref),
            (table_hbm, table_ref),
            (offsets_hbm, offsets),
            (pair_bits_hbm, pair_bits),
            (qk_hbm, qk_ref),
            (attn_rate_hbm, attn_rate_ref),
            (mlp_rate_hbm, mlp_rate_ref),
            (up_scale_hbm, up_scale_ref),
            (gate_scale_hbm, gate_scale_ref),
        )
    ):
        copy = pltpu.make_async_copy(source, target, local_sem.at[number])
        copy.start()
        loads.append(copy)

    def push(source, target, peer, hop, stride=1):
        def one(k):
            pltpu.make_async_remote_copy(
                src_ref=source(k),
                dst_ref=target(k),
                send_sem=send_sem.at[hop],
                recv_sem=recv_sem.at[hop],
                device_id=peer(k),
                device_id_type=MESH,
            ).start()

        one(N // 2)

        def pair(step, carry):
            one(N // 2 - stride * step)
            one(N // 2 + stride * step)
            return carry

        lax.fori_loop(1, N // 2 // stride, pair, 0)

    def others(ref):
        return ref.at[pl.ds(1, N - 1)]

    def gather(rows, peer, hop):
        push(lambda k: rows.at[0], lambda k: rows.at[k], peer, hop)

    sibling = my_group + 1 - 2 * lax.rem(my_group, 2)

    def gather_group(rows, hop):
        push(lambda k: rows.at[0], lambda k: rows.at[lax.div(k, 2)], group_peer, hop, 2)

    def relay_group(rows, hop, relay_hop):
        wait_for(rows.at[pl.ds(1, N // 2 - 1)], recv_sem.at[hop])
        pltpu.make_async_remote_copy(
            src_ref=rows.at[pl.ds(0, N // 2)],
            dst_ref=rows.at[pl.ds(N // 2, N // 2)],
            send_sem=send_sem.at[relay_hop],
            recv_sem=recv_sem.at[relay_hop],
            device_id=(sibling, my_shard),
            device_id_type=MESH,
        ).start()
        wait_for(rows.at[pl.ds(N // 2, N // 2)], recv_sem.at[relay_hop])

    def slot_of(group):
        back = lax.rem(my_group - group + 2 * N, N)
        sibling_back = lax.rem(sibling - group + 2 * N, N)
        odd = lax.rem(back, 2)
        return (1 - odd) * lax.div(back, 2) + odd * (N // 2 + lax.div(sibling_back, 2))

    def give_back(source, target, hop):
        push(lambda k: source.at[k], lambda k: target.at[k], lambda k: shard_peer(N - k), hop)

    for number in range(7, 11):
        loads[number].wait()
    rows2 = iota((2, 128), 0)
    lane = iota((1, 128), 1)
    length2 = jnp.where(rows2 == 0, lengths[0], lengths[1])
    in_length = iota((2, 128), 1) < length2
    keeper = jnp.where((keep_ref[...] == 1) & in_length, 1.0, 0.0)
    dropper = jnp.where((keep_ref[...] == 0) & in_length, 1.0, 0.0)
    lower = jnp.where(iota((128, 128), 0) <= iota((128, 128), 1), 1.0, 0.0).astype(BF16)
    position = jnp.dot(keeper.astype(BF16), lower, preferred_element_type=F32)
    place2 = jnp.where(keeper > 0.0, position - 1.0, -1.0)
    kept = jnp.sum(keeper, axis=1, keepdims=True)
    live2 = kept + jnp.where(jnp.sum(dropper, axis=1, keepdims=True) > 0.0, 1.0, 0.0)
    table_square = jnp.broadcast_to(table_ref[...].astype(F32), (WTAB, WTAB))
    table_column = jnp.sum(
        jnp.where(iota((WTAB, WTAB), 0) == iota((WTAB, WTAB), 1), table_square, 0.0),
        axis=1,
        keepdims=True,
    )
    target_row = iota((128, 128), 0).astype(F32)
    mixings = []
    for j in range(2):
        hit = iota((WTAB, 128), 0) == index_ref[j : j + 1, :]
        weights = (
            jnp.sum(jnp.where(hit, table_column, 0.0), axis=0, keepdims=True)
            * dropper[j : j + 1, :]
        )
        placing = jnp.where(target_row == place2[j : j + 1, :], 1.0, 0.0)
        summing = jnp.where(target_row == kept[j : j + 1, :], weights, 0.0)
        mixings.append((placing + summing).astype(BF16))
    loads[1].wait()

    def compact(part):
        columns = slice(WIDE * part, WIDE * part + WIDE)
        for j in range(2):
            result = jnp.dot(mixings[j], kv[j, :, columns], preferred_element_type=F32)
            packed[part, 8 * j : 8 * j + 8] = result.astype(BF16).reshape(8, 16, WIDE)

    compact(0)

    loads[0].wait()
    pl.semaphore_wait(barrier, 2 * (N - 1))

    gather_group(group_rows, 0)

    def spread_cache(part):
        push(
            lambda k: packed.at[part, lax.rem(my_group + k, N)],
            lambda k: arrived[part].at[k],
            group_peer,
            HOPS + part,
        )
        arrived[part][0] = packed[part, my_group]

    spread_cache(0)
    for part in range(1, PARTS):
        compact(part)
        spread_cache(part)
    for number in range(11, 18):
        loads[number].wait()

    landing_slot = lax.div(my_group, 8)
    landing_rows = pl.ds(pl.multiple_of(16 * lax.rem(my_group, 8), 16), 16)
    my_offset = offsets[0, landing_slot]
    own_chunks = []

    def deliver_cache(part):
        wait_for(others(arrived[part]), recv_sem.at[HOPS + part])
        for m in range(N):
            staged[part, m] = arrived[part][lax.rem(my_offset + N - m, N)]
        landing = cache_out.at[landing_slot, landing_rows, pl.ds(WIDE * part, WIDE)]
        def one(target, carry):
            @pl.when(target != my_group)
            def _():
                pltpu.make_async_remote_copy(
                    src_ref=staged.at[part, lax.rem(target - my_group + N, N)],
                    dst_ref=landing,
                    send_sem=send_sem.at[HOPS + PARTS + part],
                    recv_sem=recv_sem.at[HOPS + PARTS + part],
                    device_id=(target, my_shard),
                    device_id_type=MESH,
                ).start()
            return carry

        lax.fori_loop(0, N, one, 0)
        own_chunk = pltpu.make_async_copy(staged.at[part, 0], landing, local_sem.at[18 + part])
        own_chunk.start()
        own_chunks.append(own_chunk)

    relay_group(group_rows, 0, 8)
    offset0 = offsets[0, 0]
    offset1 = offsets[0, 1]
    first = iota((2, D), 0) == 0
    own_tokens = group_rows[0].astype(F32)
    moved_tokens = jnp.where(
        first,
        group_rows[slot_of(my_group + offset0)].astype(F32),
        group_rows[slot_of(my_group + offset1)].astype(F32),
    )
    shard_rows[0] = moved_tokens.astype(BF16)
    gather(shard_rows, shard_peer, 1)

    def stack(rows):
        for k in range(N):
            lhs[2 * k : 2 * k + 2, :] = rows[k].astype(F32)
        return lhs[...].astype(BF16)

    def shifter(width, frame):
        shift = lax.rem(width * my_shard, 128)
        return jnp.where(
            iota((width, frame), 1) == iota((width, frame), 0) + shift, 1.0, 0.0
        ).astype(BF16)

    def spread_back(rows, weight, width, frame, send, recv, flat, hop):
        columns = times_transposed(rows, weight).astype(BF16)
        framed = jnp.dot(columns, shifter(width, frame), preferred_element_type=F32)
        for k in range(N):
            send[k] = framed[2 * k : 2 * k + 2, :]
        recv[0] = framed[0:2, :]
        give_back(send, recv, hop)
        flat[...] = jnp.zeros(flat.shape, F32)
        wait_for(others(recv), recv_sem.at[hop])
        for c in range(N):
            begin = 128 * ((width * c) // 128)
            flat[:, begin : begin + frame] += recv[lax.rem(c + N - my_shard, N)]

    loads[2].wait()
    wait_for(others(shard_rows), recv_sem.at[1])
    spread_back(stack(shard_rows), w_qkv[...], 240, 384, qkv_send, qkv_recv, qkv_flat, 2)

    head_mask = lax.shift_right_logical(iota((HEADS_PAD, D), 1), 6) == iota((HEADS_PAD, D), 0)
    stat_row = iota((HEADS_PAD, 128), 0)
    stat_column = iota((HEADS_PAD, 128), 1)
    stat_lane = stat_column == stat_row
    stat_lane1 = stat_column == stat_row + HEADS_PAD
    stat_lane2 = stat_column == stat_row + 2 * HEADS_PAD
    stat_any = stat_lane | stat_lane1 | stat_lane2
    scaling = qk_ref[...][None, :]
    score_scale = float(DH) ** 0.5

    def heads(row):
        masked = jnp.where(head_mask, jnp.broadcast_to(row, (HEADS_PAD, D)), 0.0)
        squares = jnp.sum(masked * masked, axis=1, keepdims=True)
        return (masked * lax.rsqrt(squares + EPSILON) * scaling).astype(BF16)

    home = lax.rem(my_group + offset1, N)
    partner_here = jnp.bitwise_xor(home, pair_bits[0, 0])
    for j in range(2):
        queries = heads(qkv_flat[j : j + 1, 0:D])
        new_keys = heads(qkv_flat[j : j + 1, D : 2 * D])
        new_values = qkv_flat[j : j + 1, 2 * D : 3 * D]
        scores = sum(
            times_transposed(
                queries[:, WIDE * part : WIDE * part + WIDE],
                packed[part, 8 * j : 8 * j + 8].reshape(128, WIDE),
            )
            for part in range(KEY_PARTS)
        )
        scores = score_scale * scores
        fresh = score_scale * jnp.sum(
            queries.astype(F32) * new_keys.astype(F32), axis=1, keepdims=True
        )
        if j == 1:
            counted = jnp.full((HEADS_PAD, 1), home, jnp.int32) < partner_here
        else:
            counted = jnp.full((HEADS_PAD, 1), True)
        valid = jnp.broadcast_to(lane.astype(F32) < live2[j : j + 1, :], (HEADS_PAD, 128))
        highest = jnp.maximum(
            jnp.max(jnp.where(valid, scores, NEGATIVE), axis=1, keepdims=True),
            jnp.where(counted, fresh, NEGATIVE),
        )
        soft = jnp.where(valid, jnp.exp(jnp.where(valid, scores - highest, 0.0)), 0.0)
        fresh_weight = jnp.where(counted, jnp.exp(fresh - highest), 0.0)
        weight_sum = jnp.sum(soft, axis=1, keepdims=True) + fresh_weight
        fresh_low = fresh_weight.astype(BF16).astype(F32)
        for part in range(KEY_PARTS):
            columns = slice(WIDE * part, WIDE * part + WIDE)
            values = packed[KEY_PARTS + part, 8 * j : 8 * j + 8].reshape(128, WIDE)
            weighted = jnp.dot(soft.astype(BF16), values, preferred_element_type=F32)
            weighted = weighted + fresh_low * new_values[:, columns]
            partial_wide[j : j + 1, columns] = jnp.sum(
                jnp.where(head_mask[:, columns], weighted / weight_sum, 0.0),
                axis=0,
                keepdims=True,
            )
    total = highest + jnp.log(weight_sum)
    piece0 = total.astype(BF16).astype(F32)
    piece1 = (total - piece0).astype(BF16).astype(F32)
    piece2 = total - piece0 - piece1
    pieces = jnp.where(stat_lane, piece0, 0.0)
    pieces = pieces + jnp.where(stat_lane1, piece1, 0.0)
    pieces = pieces + jnp.where(stat_lane2, piece2, 0.0)
    partial_wide[0:1, D : D + 128] = jnp.zeros((1, 128), F32)
    partial_wide[1:2, D : D + 128] = jnp.sum(pieces, axis=0, keepdims=True)
    partial[0] = partial_wide[...].astype(BF16)

    gather_group(partial, 3)

    deliver_cache(0)

    relay_group(partial, 3, 9)
    partner = jnp.bitwise_xor(my_group, pair_bits[0, 0])
    mine = partial[slot_of(my_group - offset1)].astype(F32)[1:2, :]
    other = partial[slot_of(partner - offset1)].astype(F32)[1:2, :]

    def total_of(row):
        pieces = jnp.broadcast_to(row[:, D : D + 128], (HEADS_PAD, 128))
        return jnp.sum(jnp.where(stat_any, pieces, 0.0), axis=1, keepdims=True)

    def by_column(column):
        return jnp.sum(jnp.where(head_mask, column, 0.0), axis=0, keepdims=True)

    my_total = total_of(mine)
    other_total = total_of(other)
    merged = jnp.maximum(my_total, other_total)
    my_factor = jnp.exp(my_total - merged)
    other_factor = jnp.exp(other_total - merged)
    both = my_factor + other_factor
    long_row = mine[:, 0:D] * by_column(my_factor / both) + other[:, 0:D] * by_column(
        other_factor / both
    )
    short_row = partial[slot_of(my_group - offset0)].astype(F32)[0:1, 0:D]
    attended = jnp.where(
        first, jnp.broadcast_to(short_row, (2, D)), jnp.broadcast_to(long_row, (2, D))
    )
    attended_rows[0] = attended.astype(BF16)
    gather(attended_rows, shard_peer, 4)
    for part in range(1, PARTS):
        deliver_cache(part)

    loads[3].wait()
    wait_for(others(attended_rows), recv_sem.at[4])
    spread_back(stack(attended_rows), w_out[...], 80, 256, out_send, out_recv, out_flat, 5)
    attention_out = out_flat[:, 0:D]
    mixed = rms_normal(
        own_tokens + attn_rate_ref[...][None, :] * (rms_normal(attention_out) - own_tokens)
    )
    mixed_rows[0] = mixed.astype(BF16)
    gather(mixed_rows, shard_peer, 6)

    loads[4].wait()
    loads[5].wait()
    loads[6].wait()
    wait_for(others(mixed_rows), recv_sem.at[6])
    rows = stack(mixed_rows)
    up = times_transposed(rows, w_up[...]) * up_scale_ref[...][None, :]
    gate = times_transposed(rows, w_gate[...]) * (
        gate_scale_ref[...][None, :] * float(D) ** 0.5
    )
    inner = (up * (gate / (1.0 + jnp.exp(-gate)))).astype(BF16)
    sum_wide[...] = jnp.dot(inner, w_down[...], preferred_element_type=F32)
    for k in range(N):
        sum_send[k] = sum_wide[2 * k : 2 * k + 2, :].astype(BF16)
    sum_recv[0] = sum_send[0]
    give_back(sum_send, sum_recv, 7)
    wait_for(others(sum_recv), recv_sem.at[7])
    mlp_out = sum_recv[0].astype(F32)
    for k in range(1, N):
        mlp_out = mlp_out + sum_recv[k].astype(F32)
    hidden_out[...] = rms_normal(
        mixed + mlp_rate_ref[...][None, :] * (rms_normal(mlp_out) - mixed)
    ).astype(BF16)

    for part in range(PARTS):
        wait_for(others(staged.at[part]), recv_sem.at[HOPS + PARTS + part])
        own_chunks[part].wait()
    half = pl.ds(N // 2, N // 2)
    most = pl.ds(1, N // 2 - 1)
    sent = (
        [
            group_rows.at[most],
            others(shard_rows),
            others(qkv_recv),
            partial.at[most],
            others(attended_rows),
            others(out_recv),
            others(mixed_rows),
            others(sum_recv),
            group_rows.at[half],
            partial.at[half],
        ]
        + [others(arrived[part]) for part in range(PARTS)]
        + [others(staged.at[part]) for part in range(PARTS)]
    )
    for hop, ref in enumerate(sent):
        wait_for(ref, send_sem.at[hop])


def finish_kernel(hidden, cache, hidden_out, cache_out, sems):
    copies = [pltpu.make_async_copy(hidden, hidden_out, sems.at[0])]
    for number in range(8):
        part = (number // 4, pl.ds(32 * (number % 4), 32))
        copies.append(
            pltpu.make_async_copy(cache.at[part], cache_out.at[part], sems.at[1 + number])
        )
    for copy in copies:
        copy.start()
    for copy in copies:
        copy.wait()


def per_device(
    tokens,
    kv_cache,
    keep_list,
    lengths,
    merge_index,
    merge_table,
    move_offset,
    pair_mask,
    w_qkv,
    w_out,
    w_up,
    w_gate,
    w_down,
    qk_scale,
    attn_rate,
    mlp_rate,
    up_scale,
    gate_scale,
):
    vmem = pl.BlockSpec(memory_space=pltpu.VMEM)
    hbm = pl.BlockSpec(memory_space=pltpu.HBM)

    hidden, cache = pl.pallas_call(
        layer_kernel,
        out_shape=(
            pltpu.VMEM((2, D), BF16),
            pltpu.VMEM((2, 128, 2 * D), BF16),
        ),
        in_specs=[hbm] * 18,
        out_specs=(vmem, pl.BlockSpec(memory_space=pl.ANY)),
        scratch_shapes=[
            pltpu.SMEM((2,), jnp.int32),
            pltpu.SMEM((1, 2), jnp.int32),
            pltpu.SMEM((1, 1), jnp.int32),
            pltpu.VMEM((2, 128), jnp.int32),
            pltpu.VMEM((2, 128), jnp.int32),
            pltpu.VMEM((1, WTAB), BF16),
            pltpu.VMEM((D,), F32),
            pltpu.VMEM((D,), F32),
            pltpu.VMEM((D,), F32),
            pltpu.VMEM((320,), F32),
            pltpu.VMEM((320,), F32),
            pltpu.VMEM((2, 128, 2 * D), BF16),
            pltpu.VMEM((240, D), BF16),
            pltpu.VMEM((80, D), BF16),
            pltpu.VMEM((320, D), BF16),
            pltpu.VMEM((320, D), BF16),
            pltpu.VMEM((320, D), BF16),
            pltpu.VMEM((PARTS, N, 16, WIDE), BF16),
            [pltpu.VMEM((N, 16, WIDE), BF16)] * PARTS,
            pltpu.VMEM((PARTS, N, 16, WIDE), BF16),
            pltpu.VMEM((N, 2, D), BF16),
            pltpu.VMEM((N, 2, D), BF16),
            pltpu.VMEM((2 * N, D), F32),
            pltpu.VMEM((N, 2, 384), F32),
            pltpu.VMEM((N, 2, 384), F32),
            pltpu.VMEM((2, 3 * D + 128), F32),
            pltpu.VMEM((2, D + 128), F32),
            pltpu.VMEM((N, 2, D + 128), BF16),
            pltpu.VMEM((N, 2, D), BF16),
            pltpu.VMEM((N, 2, 256), F32),
            pltpu.VMEM((N, 2, 256), F32),
            pltpu.VMEM((2, D + 128), F32),
            pltpu.VMEM((N, 2, D), BF16),
            pltpu.VMEM((2 * N, D), F32),
            pltpu.VMEM((N, 2, D), BF16),
            pltpu.VMEM((N, 2, D), BF16),
            pltpu.SemaphoreType.DMA((18 + PARTS,)),
            pltpu.SemaphoreType.DMA((HOPS + 2 * PARTS,)),
            pltpu.SemaphoreType.DMA((HOPS + 2 * PARTS,)),
        ],
        compiler_params=pltpu.CompilerParams(
            collective_id=0, has_side_effects=True, vmem_limit_bytes=60 << 20
        ),
    )(
        lengths,
        move_offset,
        pair_mask[None, :],
        keep_list,
        merge_index,
        merge_table[None, :],
        qk_scale,
        attn_rate,
        mlp_rate,
        up_scale,
        gate_scale,
        tokens,
        kv_cache,
        w_qkv.T,
        w_out.T,
        w_up.T,
        w_gate.T,
        w_down,
    )
    return pl.pallas_call(
        finish_kernel,
        out_shape=(
            pltpu.HBM((2, D), BF16),
            pltpu.HBM((2, 128, 2 * D), BF16),
        ),
        in_specs=[pl.BlockSpec(memory_space=pl.ANY)] * 2,
        out_specs=(pl.BlockSpec(memory_space=pl.ANY),) * 2,
        scratch_shapes=[pltpu.SemaphoreType.DMA((9,))],
    )(
        pltpu.with_memory_space_constraint(hidden, pltpu.VMEM),
        pltpu.with_memory_space_constraint(cache, pltpu.VMEM),
    )


def solution(mesh):
    return jax.shard_map(
        per_device,
        mesh=mesh,
        in_specs=(
            P(("group", "shard"), None),
            P(("group", "shard"), None, None),
            P(("group", "shard"), None),
            P(("group", "shard")),
            P(("group", "shard"), None),
            P(),
            P("shard", None),
            P("shard"),
            P(None, "shard"),
            P(None, "shard"),
            P(None, "shard"),
            P(None, "shard"),
            P("shard", None),
            P(),
            P(),
            P(),
            P("shard"),
            P("shard"),
        ),
        out_specs=(P(("group", "shard"), None), P(("group", "shard"), None, None)),
        check_vma=False,
    )
```

```python
import functools
import math

import jax
import jax.numpy as jnp
from jax import lax
from jax.experimental import pallas as pl
from jax.experimental.pallas import tpu as pltpu
from jax.sharding import PartitionSpec as P

DH = 64
WTAB = 16
N = 16
D = 1280
PARTS = 4
WIDE = 2 * D // PARTS
KEY_PARTS = PARTS // 2
PIECES = D // 128
HOPS = 10
HEADS_PAD = 32
EPSILON = 1e-06
NEGATIVE = -1e30
MESH = pl.DeviceIdType.MESH
F32 = jnp.float32
BF16 = jnp.bfloat16


def iota(shape, axis):
    return lax.broadcasted_iota(jnp.int32, shape, axis)


def rms_normal(vector):
    return vector * lax.rsqrt(jnp.mean(vector * vector, axis=-1, keepdims=True) + EPSILON)


def times_transposed(rows, weight):
    return lax.dot_general(rows, weight, (((1,), (1,)), ((), ())), preferred_element_type=F32)


def wait_for(ref, sem):
    pltpu.make_async_copy(ref, ref, sem).wait()


def layer_kernel(
    lengths_hbm,
    offsets_hbm,
    pair_bits_hbm,
    keep_hbm,
    index_hbm,
    table_hbm,
    qk_hbm,
    attn_rate_hbm,
    mlp_rate_hbm,
    up_scale_hbm,
    gate_scale_hbm,
    tokens_hbm,
    kv_hbm,
    w_qkv_hbm,
    w_out_hbm,
    w_up_hbm,
    w_gate_hbm,
    w_down_hbm,
    hidden_out,
    cache_out,
    lengths,
    offsets,
    pair_bits,
    keep_ref,
    index_ref,
    table_ref,
    qk_ref,
    attn_rate_ref,
    mlp_rate_ref,
    up_scale_ref,
    gate_scale_ref,
    kv,
    w_qkv,
    w_out,
    w_up,
    w_gate,
    w_down,
    packed,
    arrived,
    staged,
    own_rows,
    piece_send,
    piece_recv,
    turn_send,
    turn_recv,
    shard_rows,
    lhs,
    qkv_send,
    qkv_recv,
    qkv_flat,
    partial_wide,
    partial,
    attended_rows,
    out_send,
    out_recv,
    out_flat,
    mixed_rows,
    sum_wide,
    sum_send,
    sum_recv,
    local_sem,
    send_sem,
    recv_sem,
):
    my_group = lax.axis_index("group")
    my_shard = lax.axis_index("shard")

    def group_peer(k):
        return (lax.rem(my_group + k, N), my_shard)

    def shard_peer(k):
        return (my_group, lax.rem(my_shard + k, N))

    barrier = pltpu.get_barrier_semaphore()

    def greet(k, carry):
        pl.semaphore_signal(barrier, inc=1, device_id=group_peer(k), device_id_type=MESH)
        pl.semaphore_signal(barrier, inc=1, device_id=shard_peer(k), device_id_type=MESH)
        return carry

    lax.fori_loop(1, N, greet, 0)

    loads = []
    for number, (source, target) in enumerate(
        (
            (tokens_hbm, own_rows),
            (kv_hbm.at[:, :, pl.ds(0, WIDE)], kv.at[:, :, pl.ds(0, WIDE)]),
            (w_qkv_hbm, w_qkv),
            (w_out_hbm, w_out),
            (w_up_hbm, w_up),
            (w_gate_hbm, w_gate),
            (w_down_hbm, w_down),
            (lengths_hbm, lengths),
            (keep_hbm, keep_ref),
            (index_hbm, index_ref),
            (table_hbm, table_ref),
            (offsets_hbm, offsets),
            (pair_bits_hbm, pair_bits),
            (qk_hbm, qk_ref),
            (attn_rate_hbm, attn_rate_ref),
            (mlp_rate_hbm, mlp_rate_ref),
            (up_scale_hbm, up_scale_ref),
            (gate_scale_hbm, gate_scale_ref),
        )
    ):
        copy = pltpu.make_async_copy(source, target, local_sem.at[number])
        copy.start()
        loads.append(copy)
    rest_of_kv = pltpu.make_async_copy(
        kv_hbm.at[:, :, pl.ds(WIDE, 2 * D - WIDE)],
        kv.at[:, :, pl.ds(WIDE, 2 * D - WIDE)],
        local_sem.at[18 + PARTS],
    )
    rest_of_kv.start()

    def push(source, target, peer, hop, stride=1):
        def one(k):
            pltpu.make_async_remote_copy(
                src_ref=source(k),
                dst_ref=target(k),
                send_sem=send_sem.at[hop],
                recv_sem=recv_sem.at[hop],
                device_id=peer(k),
                device_id_type=MESH,
            ).start()

        one(N // 2)

        def pair(step, carry):
            one(N // 2 - stride * step)
            one(N // 2 + stride * step)
            return carry

        lax.fori_loop(1, N // 2 // stride, pair, 0)

    def others(ref):
        return ref.at[pl.ds(1, N - 1)]

    def gather(rows, peer, hop):
        push(lambda k: rows.at[0], lambda k: rows.at[k], peer, hop)

    sibling = my_group + 1 - 2 * lax.rem(my_group, 2)

    def gather_group(rows, hop):
        push(lambda k: rows.at[0], lambda k: rows.at[lax.div(k, 2)], group_peer, hop, 2)

    def relay_group(rows, hop, relay_hop):
        wait_for(rows.at[pl.ds(1, N // 2 - 1)], recv_sem.at[hop])
        pltpu.make_async_remote_copy(
            src_ref=rows.at[pl.ds(0, N // 2)],
            dst_ref=rows.at[pl.ds(N // 2, N // 2)],
            send_sem=send_sem.at[relay_hop],
            recv_sem=recv_sem.at[relay_hop],
            device_id=(sibling, my_shard),
            device_id_type=MESH,
        ).start()
        wait_for(rows.at[pl.ds(N // 2, N // 2)], recv_sem.at[relay_hop])

    def slot_of(group):
        back = lax.rem(my_group - group + 2 * N, N)
        sibling_back = lax.rem(sibling - group + 2 * N, N)
        odd = lax.rem(back, 2)
        return (1 - odd) * lax.div(back, 2) + odd * (N // 2 + lax.div(sibling_back, 2))

    def give_back(source, target, hop):
        push(lambda k: source.at[k], lambda k: target.at[k], lambda k: shard_peer(N - k), hop)

    for number in range(7, 11):
        loads[number].wait()
    rows2 = iota((2, 128), 0)
    lane = iota((1, 128), 1)
    length2 = jnp.where(rows2 == 0, lengths[0], lengths[1])
    in_length = iota((2, 128), 1) < length2
    keeper = jnp.where((keep_ref[...] == 1) & in_length, 1.0, 0.0)
    dropper = jnp.where((keep_ref[...] == 0) & in_length, 1.0, 0.0)
    lower = jnp.where(iota((128, 128), 0) <= iota((128, 128), 1), 1.0, 0.0).astype(BF16)
    position = jnp.dot(keeper.astype(BF16), lower, preferred_element_type=F32)
    place2 = jnp.where(keeper > 0.0, position - 1.0, -1.0)
    kept = jnp.sum(keeper, axis=1, keepdims=True)
    live2 = kept + jnp.where(jnp.sum(dropper, axis=1, keepdims=True) > 0.0, 1.0, 0.0)
    table_square = jnp.broadcast_to(table_ref[...].astype(F32), (WTAB, WTAB))
    table_column = jnp.sum(
        jnp.where(iota((WTAB, WTAB), 0) == iota((WTAB, WTAB), 1), table_square, 0.0),
        axis=1,
        keepdims=True,
    )
    target_row = iota((128, 128), 0).astype(F32)
    mixings = []
    for j in range(2):
        hit = iota((WTAB, 128), 0) == index_ref[j : j + 1, :]
        weights = (
            jnp.sum(jnp.where(hit, table_column, 0.0), axis=0, keepdims=True)
            * dropper[j : j + 1, :]
        )
        placing = jnp.where(target_row == place2[j : j + 1, :], 1.0, 0.0)
        summing = jnp.where(target_row == kept[j : j + 1, :], weights, 0.0)
        mixings.append((placing + summing).astype(BF16))
    loads[1].wait()

    def compact(part):
        columns = slice(WIDE * part, WIDE * part + WIDE)
        for j in range(2):
            result = jnp.dot(mixings[j], kv[j, :, columns], preferred_element_type=F32)
            packed[part, 8 * j : 8 * j + 8] = result.astype(BF16).reshape(8, 16, WIDE)

    compact(0)

    loads[0].wait()
    for piece in range(PIECES):
        columns = slice(128 * piece, 128 * piece + 128)
        piece_send[(piece + PIECES // 2) % PIECES] = own_rows[:, columns]
        if piece == PIECES // 2:
            piece_recv[0] = own_rows[:, columns]
    pl.semaphore_wait(barrier, 2 * (N - 1))

    for slot in range(1, PIECES):
        distance = slot if slot < PIECES // 2 else slot - PIECES
        pltpu.make_async_remote_copy(
            src_ref=piece_send.at[slot],
            dst_ref=piece_recv.at[slot],
            send_sem=send_sem.at[0],
            recv_sem=recv_sem.at[0],
            device_id=group_peer(distance + N),
            device_id_type=MESH,
        ).start()

    def spread_cache(part):
        push(
            lambda k: packed.at[part, lax.rem(my_group + k, N)],
            lambda k: arrived[part].at[k],
            group_peer,
            HOPS + part,
        )
        arrived[part][0] = packed[part, my_group]

    spread_cache(0)
    rest_of_kv.wait()
    for part in range(1, PARTS):
        compact(part)
    for number in range(11, 18):
        loads[number].wait()

    offset0 = offsets[0, 0]
    offset1 = offsets[0, 1]
    narrow = iota((2, 128), 0) == 0
    wait_for(piece_recv.at[pl.ds(1, PIECES - 1)], recv_sem.at[0])

    def piece_for(m, offset):
        piece = lax.rem(PIECES // 2 - m - offset + 2 * N, N)
        slot = lax.rem(jnp.minimum(piece, PIECES - 1) + PIECES // 2, PIECES)
        return piece_recv[slot].astype(F32)

    for m in range(N):
        turned = jnp.where(narrow, piece_for(m, offset0), piece_for(m, offset1))
        turn_send[m] = turned.astype(BF16)
    turn_recv[0] = turn_send[0]
    push(lambda k: turn_send.at[k], lambda k: turn_recv.at[k], group_peer, 8)
    spread_cache(1)
    spread_cache(2)

    landing_slot = lax.div(my_group, 8)
    landing_rows = pl.ds(pl.multiple_of(16 * lax.rem(my_group, 8), 16), 16)
    my_offset = offsets[0, landing_slot]
    own_chunks = []

    def deliver_cache(part):
        wait_for(others(arrived[part]), recv_sem.at[HOPS + part])
        landing = cache_out.at[landing_slot, landing_rows, pl.ds(WIDE * part, WIDE)]
        def one(target, carry):
            m = lax.rem(target - my_group + N, N)
            staged[part, m] = arrived[part][lax.rem(my_offset + N - m, N)]

            @pl.when(target != my_group)
            def _():
                pltpu.make_async_remote_copy(
                    src_ref=staged.at[part, m],
                    dst_ref=landing,
                    send_sem=send_sem.at[HOPS + PARTS + part],
                    recv_sem=recv_sem.at[HOPS + PARTS + part],
                    device_id=(target, my_shard),
                    device_id_type=MESH,
                ).start()
            return carry

        lax.fori_loop(0, N, one, 0)
        own_chunk = pltpu.make_async_copy(staged.at[part, 0], landing, local_sem.at[18 + part])
        own_chunk.start()
        own_chunks.append(own_chunk)

    first = iota((2, D), 0) == 0
    own_tokens = own_rows[...].astype(F32)
    wait_for(others(turn_recv), recv_sem.at[8])
    for piece in range(PIECES):
        back = PIECES // 2 - piece + 2 * N
        moved = jnp.where(
            narrow,
            turn_recv[lax.rem(back - offset0, N)].astype(F32),
            turn_recv[lax.rem(back - offset1, N)].astype(F32),
        )
        shard_rows[0, :, 128 * piece : 128 * piece + 128] = moved.astype(BF16)
    gather(shard_rows, shard_peer, 1)

    def stack(rows):
        for k in range(N):
            lhs[2 * k : 2 * k + 2, :] = rows[k].astype(F32)
        return lhs[...].astype(BF16)

    def shifter(width, frame):
        shift = lax.rem(width * my_shard, 128)
        return jnp.where(
            iota((width, frame), 1) == iota((width, frame), 0) + shift, 1.0, 0.0
        ).astype(BF16)

    def spread_back(rows, weight, width, frame, send, recv, flat, hop):
        columns = times_transposed(rows, weight).astype(BF16)
        framed = jnp.dot(columns, shifter(width, frame), preferred_element_type=F32)
        for k in range(N):
            send[k] = framed[2 * k : 2 * k + 2, :]
        recv[0] = framed[0:2, :]
        give_back(send, recv, hop)
        flat[...] = jnp.zeros(flat.shape, F32)
        wait_for(others(recv), recv_sem.at[hop])
        for c in range(N):
            begin = 128 * ((width * c) // 128)
            flat[:, begin : begin + frame] += recv[lax.rem(c + N - my_shard, N)]

    loads[2].wait()
    wait_for(others(shard_rows), recv_sem.at[1])
    spread_cache(3)
    spread_back(stack(shard_rows), w_qkv[...], 240, 384, qkv_send, qkv_recv, qkv_flat, 2)

    head_mask = lax.shift_right_logical(iota((HEADS_PAD, D), 1), 6) == iota((HEADS_PAD, D), 0)
    stat_row = iota((HEADS_PAD, 128), 0)
    stat_column = iota((HEADS_PAD, 128), 1)
    stat_lane = stat_column == stat_row
    stat_lane1 = stat_column == stat_row + HEADS_PAD
    stat_lane2 = stat_column == stat_row + 2 * HEADS_PAD
    stat_any = stat_lane | stat_lane1 | stat_lane2
    scaling = qk_ref[...][None, :]
    score_scale = float(DH) ** 0.5

    def heads(row):
        masked = jnp.where(head_mask, jnp.broadcast_to(row, (HEADS_PAD, D)), 0.0)
        squares = jnp.sum(masked * masked, axis=1, keepdims=True)
        return (masked * lax.rsqrt(squares + EPSILON) * scaling).astype(BF16)

    home = lax.rem(my_group + offset1, N)
    partner_here = jnp.bitwise_xor(home, pair_bits[0, 0])
    for j in range(2):
        queries = heads(qkv_flat[j : j + 1, 0:D])
        new_keys = heads(qkv_flat[j : j + 1, D : 2 * D])
        new_values = qkv_flat[j : j + 1, 2 * D : 3 * D]
        scores = sum(
            times_transposed(
                queries[:, WIDE * part : WIDE * part + WIDE],
                packed[part, 8 * j : 8 * j + 8].reshape(128, WIDE),
            )
            for part in range(KEY_PARTS)
        )
        scores = score_scale * scores
        fresh = score_scale * jnp.sum(
            queries.astype(F32) * new_keys.astype(F32), axis=1, keepdims=True
        )
        if j == 1:
            counted = jnp.full((HEADS_PAD, 1), home, jnp.int32) < partner_here
        else:
            counted = jnp.full((HEADS_PAD, 1), True)
        valid = jnp.broadcast_to(lane.astype(F32) < live2[j : j + 1, :], (HEADS_PAD, 128))
        highest = jnp.maximum(
            jnp.max(jnp.where(valid, scores, NEGATIVE), axis=1, keepdims=True),
            jnp.where(counted, fresh, NEGATIVE),
        )
        soft = jnp.where(valid, jnp.exp(jnp.where(valid, scores - highest, 0.0)), 0.0)
        fresh_weight = jnp.where(counted, jnp.exp(fresh - highest), 0.0)
        weight_sum = jnp.sum(soft, axis=1, keepdims=True) + fresh_weight
        fresh_low = fresh_weight.astype(BF16).astype(F32)
        for part in range(KEY_PARTS):
            columns = slice(WIDE * part, WIDE * part + WIDE)
            values = packed[KEY_PARTS + part, 8 * j : 8 * j + 8].reshape(128, WIDE)
            weighted = jnp.dot(soft.astype(BF16), values, preferred_element_type=F32)
            weighted = weighted + fresh_low * new_values[:, columns]
            partial_wide[j : j + 1, columns] = jnp.sum(
                jnp.where(head_mask[:, columns], weighted / weight_sum, 0.0),
                axis=0,
                keepdims=True,
            )
    total = highest + jnp.log(weight_sum)
    piece0 = total.astype(BF16).astype(F32)
    piece1 = (total - piece0).astype(BF16).astype(F32)
    piece2 = total - piece0 - piece1
    pieces = jnp.where(stat_lane, piece0, 0.0)
    pieces = pieces + jnp.where(stat_lane1, piece1, 0.0)
    pieces = pieces + jnp.where(stat_lane2, piece2, 0.0)
    partial_wide[0:1, D : D + 128] = jnp.zeros((1, 128), F32)
    partial_wide[1:2, D : D + 128] = jnp.sum(pieces, axis=0, keepdims=True)
    partial[0] = partial_wide[...].astype(BF16)

    gather_group(partial, 3)

    for part in range(3):
        deliver_cache(part)

    relay_group(partial, 3, 9)
    partner = jnp.bitwise_xor(my_group, pair_bits[0, 0])
    mine = partial[slot_of(my_group - offset1)].astype(F32)[1:2, :]
    other = partial[slot_of(partner - offset1)].astype(F32)[1:2, :]

    def total_of(row):
        pieces = jnp.broadcast_to(row[:, D : D + 128], (HEADS_PAD, 128))
        return jnp.sum(jnp.where(stat_any, pieces, 0.0), axis=1, keepdims=True)

    def by_column(column):
        return jnp.sum(jnp.where(head_mask, column, 0.0), axis=0, keepdims=True)

    my_total = total_of(mine)
    other_total = total_of(other)
    merged = jnp.maximum(my_total, other_total)
    my_factor = jnp.exp(my_total - merged)
    other_factor = jnp.exp(other_total - merged)
    both = my_factor + other_factor
    long_row = mine[:, 0:D] * by_column(my_factor / both) + other[:, 0:D] * by_column(
        other_factor / both
    )
    short_row = partial[slot_of(my_group - offset0)].astype(F32)[0:1, 0:D]
    attended = jnp.where(
        first, jnp.broadcast_to(short_row, (2, D)), jnp.broadcast_to(long_row, (2, D))
    )
    attended_rows[0] = attended.astype(BF16)
    gather(attended_rows, shard_peer, 4)
    deliver_cache(3)

    loads[3].wait()
    wait_for(others(attended_rows), recv_sem.at[4])
    spread_back(stack(attended_rows), w_out[...], 80, 256, out_send, out_recv, out_flat, 5)
    attention_out = out_flat[:, 0:D]
    mixed = rms_normal(
        own_tokens + attn_rate_ref[...][None, :] * (rms_normal(attention_out) - own_tokens)
    )
    mixed_rows[0] = mixed.astype(BF16)
    gather(mixed_rows, shard_peer, 6)

    loads[4].wait()
    loads[5].wait()
    loads[6].wait()
    wait_for(others(mixed_rows), recv_sem.at[6])
    rows = stack(mixed_rows)
    up = times_transposed(rows, w_up[...]) * up_scale_ref[...][None, :]
    gate = times_transposed(rows, w_gate[...]) * (
        gate_scale_ref[...][None, :] * float(D) ** 0.5
    )
    inner = (up * (gate / (1.0 + jnp.exp(-gate)))).astype(BF16)
    sum_wide[...] = jnp.dot(inner, w_down[...], preferred_element_type=F32)
    for k in range(N):
        sum_send[k] = sum_wide[2 * k : 2 * k + 2, :].astype(BF16)
    sum_recv[0] = sum_send[0]
    give_back(sum_send, sum_recv, 7)
    wait_for(others(sum_recv), recv_sem.at[7])
    mlp_out = sum_recv[0].astype(F32)
    for k in range(1, N):
        mlp_out = mlp_out + sum_recv[k].astype(F32)
    hidden_out[...] = rms_normal(
        mixed + mlp_rate_ref[...][None, :] * (rms_normal(mlp_out) - mixed)
    ).astype(BF16)

    for part in range(PARTS):
        wait_for(others(staged.at[part]), recv_sem.at[HOPS + PARTS + part])
        own_chunks[part].wait()
    half = pl.ds(N // 2, N // 2)
    most = pl.ds(1, N // 2 - 1)
    sent = (
        [
            piece_recv.at[pl.ds(1, PIECES - 1)],
            others(shard_rows),
            others(qkv_recv),
            partial.at[most],
            others(attended_rows),
            others(out_recv),
            others(mixed_rows),
            others(sum_recv),
            others(turn_recv),
            partial.at[half],
        ]
        + [others(arrived[part]) for part in range(PARTS)]
        + [others(staged.at[part]) for part in range(PARTS)]
    )
    for hop, ref in enumerate(sent):
        wait_for(ref, send_sem.at[hop])


def finish_kernel(hidden, cache, hidden_out, cache_out, sems):
    copies = [pltpu.make_async_copy(hidden, hidden_out, sems.at[0])]
    for number in range(8):
        part = (number // 4, pl.ds(32 * (number % 4), 32))
        copies.append(
            pltpu.make_async_copy(cache.at[part], cache_out.at[part], sems.at[1 + number])
        )
    for copy in copies:
        copy.start()
    for copy in copies:
        copy.wait()


def per_device(
    tokens,
    kv_cache,
    keep_list,
    lengths,
    merge_index,
    merge_table,
    move_offset,
    pair_mask,
    w_qkv,
    w_out,
    w_up,
    w_gate,
    w_down,
    qk_scale,
    attn_rate,
    mlp_rate,
    up_scale,
    gate_scale,
):
    vmem = pl.BlockSpec(memory_space=pltpu.VMEM)
    hbm = pl.BlockSpec(memory_space=pltpu.HBM)

    hidden, cache = pl.pallas_call(
        layer_kernel,
        out_shape=(
            pltpu.VMEM((2, D), BF16),
            pltpu.VMEM((2, 128, 2 * D), BF16),
        ),
        in_specs=[hbm] * 18,
        out_specs=(vmem, pl.BlockSpec(memory_space=pl.ANY)),
        scratch_shapes=[
            pltpu.SMEM((2,), jnp.int32),
            pltpu.SMEM((1, 2), jnp.int32),
            pltpu.SMEM((1, 1), jnp.int32),
            pltpu.VMEM((2, 128), jnp.int32),
            pltpu.VMEM((2, 128), jnp.int32),
            pltpu.VMEM((1, WTAB), BF16),
            pltpu.VMEM((D,), F32),
            pltpu.VMEM((D,), F32),
            pltpu.VMEM((D,), F32),
            pltpu.VMEM((320,), F32),
            pltpu.VMEM((320,), F32),
            pltpu.VMEM((2, 128, 2 * D), BF16),
            pltpu.VMEM((240, D), BF16),
            pltpu.VMEM((80, D), BF16),
            pltpu.VMEM((320, D), BF16),
            pltpu.VMEM((320, D), BF16),
            pltpu.VMEM((320, D), BF16),
            pltpu.VMEM((PARTS, N, 16, WIDE), BF16),
            [pltpu.VMEM((N, 16, WIDE), BF16)] * PARTS,
            pltpu.VMEM((PARTS, N, 16, WIDE), BF16),
            pltpu.VMEM((2, D), BF16),
            pltpu.VMEM((PIECES, 2, 128), BF16),
            pltpu.VMEM((PIECES, 2, 128), BF16),
            pltpu.VMEM((N, 2, 128), BF16),
            pltpu.VMEM((N, 2, 128), BF16),
            pltpu.VMEM((N, 2, D), BF16),
            pltpu.VMEM((2 * N, D), F32),
            pltpu.VMEM((N, 2, 384), F32),
            pltpu.VMEM((N, 2, 384), F32),
            pltpu.VMEM((2, 3 * D + 128), F32),
            pltpu.VMEM((2, D + 128), F32),
            pltpu.VMEM((N, 2, D + 128), BF16),
            pltpu.VMEM((N, 2, D), BF16),
            pltpu.VMEM((N, 2, 256), F32),
            pltpu.VMEM((N, 2, 256), F32),
            pltpu.VMEM((2, D + 128), F32),
            pltpu.VMEM((N, 2, D), BF16),
            pltpu.VMEM((2 * N, D), F32),
            pltpu.VMEM((N, 2, D), BF16),
            pltpu.VMEM((N, 2, D), BF16),
            pltpu.SemaphoreType.DMA((19 + PARTS,)),
            pltpu.SemaphoreType.DMA((HOPS + 2 * PARTS,)),
            pltpu.SemaphoreType.DMA((HOPS + 2 * PARTS,)),
        ],
        compiler_params=pltpu.CompilerParams(
            collective_id=0, has_side_effects=True, vmem_limit_bytes=60 << 20
        ),
    )(
        lengths,
        move_offset,
        pair_mask[None, :],
        keep_list,
        merge_index,
        merge_table[None, :],
        qk_scale,
        attn_rate,
        mlp_rate,
        up_scale,
        gate_scale,
        tokens,
        kv_cache,
        w_qkv.T,
        w_out.T,
        w_up.T,
        w_gate.T,
        w_down,
    )
    return pl.pallas_call(
        finish_kernel,
        out_shape=(
            pltpu.HBM((2, D), BF16),
            pltpu.HBM((2, 128, 2 * D), BF16),
        ),
        in_specs=[pl.BlockSpec(memory_space=pl.ANY)] * 2,
        out_specs=(pl.BlockSpec(memory_space=pl.ANY),) * 2,
        scratch_shapes=[pltpu.SemaphoreType.DMA((9,))],
    )(
        pltpu.with_memory_space_constraint(hidden, pltpu.VMEM),
        pltpu.with_memory_space_constraint(cache, pltpu.VMEM),
    )


def solution(mesh):
    return jax.shard_map(
        per_device,
        mesh=mesh,
        in_specs=(
            P(("group", "shard"), None),
            P(("group", "shard"), None, None),
            P(("group", "shard"), None),
            P(("group", "shard")),
            P(("group", "shard"), None),
            P(),
            P("shard", None),
            P("shard"),
            P(None, "shard"),
            P(None, "shard"),
            P(None, "shard"),
            P(None, "shard"),
            P("shard", None),
            P(),
            P(),
            P(),
            P("shard"),
            P("shard"),
        ),
        out_specs=(P(("group", "shard"), None), P(("group", "shard"), None, None)),
        check_vma=False,
    )
```

```python
import functools
import math

import jax
import jax.numpy as jnp
from jax import lax
from jax.experimental import pallas as pl
from jax.experimental.pallas import tpu as pltpu
from jax.sharding import PartitionSpec as P

DH = 64
WTAB = 16
N = 16
D = 1280
PARTS = 4
WIDE = 2 * D // PARTS
KEY_PARTS = PARTS // 2
PIECES = D // 128
HOPS = 10
HEADS_PAD = 32
EPSILON = 1e-06
NEGATIVE = -1e30
MESH = pl.DeviceIdType.MESH
F32 = jnp.float32
BF16 = jnp.bfloat16


def iota(shape, axis):
    return lax.broadcasted_iota(jnp.int32, shape, axis)


def rms_normal(vector):
    return vector * lax.rsqrt(jnp.mean(vector * vector, axis=-1, keepdims=True) + EPSILON)


def times_transposed(rows, weight):
    return lax.dot_general(rows, weight, (((1,), (1,)), ((), ())), preferred_element_type=F32)


def wait_for(ref, sem):
    pltpu.make_async_copy(ref, ref, sem).wait()


def layer_kernel(
    lengths_hbm,
    offsets_hbm,
    pair_bits_hbm,
    keep_hbm,
    index_hbm,
    table_hbm,
    qk_hbm,
    attn_rate_hbm,
    mlp_rate_hbm,
    up_scale_hbm,
    gate_scale_hbm,
    tokens_hbm,
    kv_hbm,
    w_qkv_hbm,
    w_out_hbm,
    w_up_hbm,
    w_gate_hbm,
    w_down_hbm,
    hidden_out,
    cache_out,
    lengths,
    offsets,
    pair_bits,
    keep_ref,
    index_ref,
    table_ref,
    qk_ref,
    attn_rate_ref,
    mlp_rate_ref,
    up_scale_ref,
    gate_scale_ref,
    kv,
    w_qkv,
    w_out,
    w_up,
    w_gate,
    w_down,
    packed,
    arrived,
    staged,
    own_rows,
    piece_send,
    piece_recv,
    turn_send,
    turn_recv,
    shard_rows,
    lhs,
    qkv_send,
    qkv_recv,
    qkv_flat,
    partial_wide,
    partial,
    attended_rows,
    out_send,
    out_recv,
    out_flat,
    mixed_rows,
    sum_wide,
    sum_send,
    sum_recv,
    local_sem,
    send_sem,
    recv_sem,
):
    my_group = lax.axis_index("group")
    my_shard = lax.axis_index("shard")

    def group_peer(k):
        return (lax.rem(my_group + k, N), my_shard)

    def shard_peer(k):
        return (my_group, lax.rem(my_shard + k, N))

    barrier = pltpu.get_barrier_semaphore()

    def greet(k, carry):
        pl.semaphore_signal(barrier, inc=1, device_id=group_peer(k), device_id_type=MESH)
        pl.semaphore_signal(barrier, inc=1, device_id=shard_peer(k), device_id_type=MESH)
        return carry

    lax.fori_loop(1, N, greet, 0)

    loads = []
    for number, (source, target) in enumerate(
        (
            (tokens_hbm, own_rows),
            (kv_hbm.at[:, :, pl.ds(0, WIDE)], kv.at[:, :, pl.ds(0, WIDE)]),
            (w_qkv_hbm, w_qkv),
            (w_out_hbm, w_out),
            (w_up_hbm, w_up),
            (w_gate_hbm, w_gate),
            (w_down_hbm, w_down),
            (lengths_hbm, lengths),
            (keep_hbm, keep_ref),
            (index_hbm, index_ref),
            (table_hbm, table_ref),
            (offsets_hbm, offsets),
            (pair_bits_hbm, pair_bits),
            (qk_hbm, qk_ref),
            (attn_rate_hbm, attn_rate_ref),
            (mlp_rate_hbm, mlp_rate_ref),
            (up_scale_hbm, up_scale_ref),
            (gate_scale_hbm, gate_scale_ref),
        )
    ):
        copy = pltpu.make_async_copy(source, target, local_sem.at[number])
        loads.append(copy)
    for number in (7, 8, 9, 10, 0, 1):
        loads[number].start()
    rest_of_kv = pltpu.make_async_copy(
        kv_hbm.at[:, :, pl.ds(WIDE, 2 * D - WIDE)],
        kv.at[:, :, pl.ds(WIDE, 2 * D - WIDE)],
        local_sem.at[18 + PARTS],
    )
    rest_of_kv.start()
    for number in (11, 12, 13, 14, 15, 16, 17, 2, 3, 4, 5, 6):
        loads[number].start()

    def push(source, target, peer, hop, stride=1):
        def one(k):
            pltpu.make_async_remote_copy(
                src_ref=source(k),
                dst_ref=target(k),
                send_sem=send_sem.at[hop],
                recv_sem=recv_sem.at[hop],
                device_id=peer(k),
                device_id_type=MESH,
            ).start()

        one(N // 2)

        def pair(step, carry):
            one(N // 2 - stride * step)
            one(N // 2 + stride * step)
            return carry

        lax.fori_loop(1, N // 2 // stride, pair, 0)

    def others(ref):
        return ref.at[pl.ds(1, N - 1)]

    def gather(rows, peer, hop):
        push(lambda k: rows.at[0], lambda k: rows.at[k], peer, hop)

    sibling = my_group + 1 - 2 * lax.rem(my_group, 2)

    def gather_group(rows, hop):
        push(lambda k: rows.at[0], lambda k: rows.at[lax.div(k, 2)], group_peer, hop, 2)

    def relay_group(rows, hop, relay_hop):
        wait_for(rows.at[pl.ds(1, N // 2 - 1)], recv_sem.at[hop])
        pltpu.make_async_remote_copy(
            src_ref=rows.at[pl.ds(0, N // 2)],
            dst_ref=rows.at[pl.ds(N // 2, N // 2)],
            send_sem=send_sem.at[relay_hop],
            recv_sem=recv_sem.at[relay_hop],
            device_id=(sibling, my_shard),
            device_id_type=MESH,
        ).start()
        wait_for(rows.at[pl.ds(N // 2, N // 2)], recv_sem.at[relay_hop])

    def slot_of(group):
        back = lax.rem(my_group - group + 2 * N, N)
        sibling_back = lax.rem(sibling - group + 2 * N, N)
        odd = lax.rem(back, 2)
        return (1 - odd) * lax.div(back, 2) + odd * (N // 2 + lax.div(sibling_back, 2))

    def give_back(source, target, hop):
        push(lambda k: source.at[k], lambda k: target.at[k], lambda k: shard_peer(N - k), hop)

    for number in range(7, 11):
        loads[number].wait()
    rows2 = iota((2, 128), 0)
    lane = iota((1, 128), 1)
    length2 = jnp.where(rows2 == 0, lengths[0], lengths[1])
    in_length = iota((2, 128), 1) < length2
    keeper = jnp.where((keep_ref[...] == 1) & in_length, 1.0, 0.0)
    dropper = jnp.where((keep_ref[...] == 0) & in_length, 1.0, 0.0)
    lower = jnp.where(iota((128, 128), 0) <= iota((128, 128), 1), 1.0, 0.0).astype(BF16)
    position = jnp.dot(keeper.astype(BF16), lower, preferred_element_type=F32)
    place2 = jnp.where(keeper > 0.0, position - 1.0, -1.0)
    kept = jnp.sum(keeper, axis=1, keepdims=True)
    live2 = kept + jnp.where(jnp.sum(dropper, axis=1, keepdims=True) > 0.0, 1.0, 0.0)
    table_square = jnp.broadcast_to(table_ref[...].astype(F32), (WTAB, WTAB))
    table_column = jnp.sum(
        jnp.where(iota((WTAB, WTAB), 0) == iota((WTAB, WTAB), 1), table_square, 0.0),
        axis=1,
        keepdims=True,
    )
    target_row = iota((128, 128), 0).astype(F32)
    mixings = []
    for j in range(2):
        hit = iota((WTAB, 128), 0) == index_ref[j : j + 1, :]
        weights = (
            jnp.sum(jnp.where(hit, table_column, 0.0), axis=0, keepdims=True)
            * dropper[j : j + 1, :]
        )
        placing = jnp.where(target_row == place2[j : j + 1, :], 1.0, 0.0)
        summing = jnp.where(target_row == kept[j : j + 1, :], weights, 0.0)
        mixings.append((placing + summing).astype(BF16))
    loads[1].wait()

    def compact(part):
        columns = slice(WIDE * part, WIDE * part + WIDE)
        for j in range(2):
            result = jnp.dot(mixings[j], kv[j, :, columns], preferred_element_type=F32)
            packed[part, 8 * j : 8 * j + 8] = result.astype(BF16).reshape(8, 16, WIDE)

    compact(0)

    loads[0].wait()
    for piece in range(PIECES):
        columns = slice(128 * piece, 128 * piece + 128)
        piece_send[(piece + PIECES // 2) % PIECES] = own_rows[:, columns]
        if piece == PIECES // 2:
            piece_recv[0] = own_rows[:, columns]
    pl.semaphore_wait(barrier, 2 * (N - 1))

    for slot in range(1, PIECES):
        distance = slot if slot < PIECES // 2 else slot - PIECES
        pltpu.make_async_remote_copy(
            src_ref=piece_send.at[slot],
            dst_ref=piece_recv.at[slot],
            send_sem=send_sem.at[0],
            recv_sem=recv_sem.at[0],
            device_id=group_peer(distance + N),
            device_id_type=MESH,
        ).start()

    def spread_cache(part):
        push(
            lambda k: packed.at[part, lax.rem(my_group + k, N)],
            lambda k: arrived[part].at[k],
            group_peer,
            HOPS + part,
        )
        arrived[part][0] = packed[part, my_group]

    spread_cache(0)
    rest_of_kv.wait()
    for part in range(1, PARTS):
        compact(part)
    for number in range(11, 18):
        loads[number].wait()

    offset0 = offsets[0, 0]
    offset1 = offsets[0, 1]
    narrow = iota((2, 128), 0) == 0
    wait_for(piece_recv.at[pl.ds(1, PIECES - 1)], recv_sem.at[0])

    def piece_for(m, offset):
        piece = lax.rem(PIECES // 2 - m - offset + 2 * N, N)
        slot = lax.rem(jnp.minimum(piece, PIECES - 1) + PIECES // 2, PIECES)
        return piece_recv[slot].astype(F32)

    for m in range(N):
        turned = jnp.where(narrow, piece_for(m, offset0), piece_for(m, offset1))
        turn_send[m] = turned.astype(BF16)
    turn_recv[0] = turn_send[0]
    push(lambda k: turn_send.at[k], lambda k: turn_recv.at[k], group_peer, 8)
    spread_cache(1)
    spread_cache(2)

    landing_slot = lax.div(my_group, 8)
    landing_rows = pl.ds(pl.multiple_of(16 * lax.rem(my_group, 8), 16), 16)
    my_offset = offsets[0, landing_slot]
    own_chunks = []

    def deliver_cache(part):
        wait_for(others(arrived[part]), recv_sem.at[HOPS + part])
        landing = cache_out.at[landing_slot, landing_rows, pl.ds(WIDE * part, WIDE)]
        def one(target, carry):
            m = lax.rem(target - my_group + N, N)
            staged[part, m] = arrived[part][lax.rem(my_offset + N - m, N)]

            @pl.when(target != my_group)
            def _():
                pltpu.make_async_remote_copy(
                    src_ref=staged.at[part, m],
                    dst_ref=landing,
                    send_sem=send_sem.at[HOPS + PARTS + part],
                    recv_sem=recv_sem.at[HOPS + PARTS + part],
                    device_id=(target, my_shard),
                    device_id_type=MESH,
                ).start()
            return carry

        lax.fori_loop(0, N, one, 0)
        own_chunk = pltpu.make_async_copy(staged.at[part, 0], landing, local_sem.at[18 + part])
        own_chunk.start()
        own_chunks.append(own_chunk)

    first = iota((2, D), 0) == 0
    own_tokens = own_rows[...].astype(F32)
    wait_for(others(turn_recv), recv_sem.at[8])
    for piece in range(PIECES):
        back = PIECES // 2 - piece + 2 * N
        moved = jnp.where(
            narrow,
            turn_recv[lax.rem(back - offset0, N)].astype(F32),
            turn_recv[lax.rem(back - offset1, N)].astype(F32),
        )
        shard_rows[0, :, 128 * piece : 128 * piece + 128] = moved.astype(BF16)
    gather(shard_rows, shard_peer, 1)

    def stack(rows):
        for k in range(N):
            lhs[2 * k : 2 * k + 2, :] = rows[k].astype(F32)
        return lhs[...].astype(BF16)

    def shifter(width, frame):
        shift = lax.rem(width * my_shard, 128)
        return jnp.where(
            iota((width, frame), 1) == iota((width, frame), 0) + shift, 1.0, 0.0
        ).astype(BF16)

    def spread_back(rows, weight, width, frame, send, recv, flat, hop):
        columns = times_transposed(rows, weight).astype(BF16)
        framed = jnp.dot(columns, shifter(width, frame), preferred_element_type=F32)
        for k in range(N):
            send[k] = framed[2 * k : 2 * k + 2, :]
        recv[0] = framed[0:2, :]
        give_back(send, recv, hop)
        flat[...] = jnp.zeros(flat.shape, F32)
        wait_for(others(recv), recv_sem.at[hop])
        for c in range(N):
            begin = 128 * ((width * c) // 128)
            flat[:, begin : begin + frame] += recv[lax.rem(c + N - my_shard, N)]

    loads[2].wait()
    wait_for(others(shard_rows), recv_sem.at[1])
    spread_cache(3)
    spread_back(stack(shard_rows), w_qkv[...], 240, 384, qkv_send, qkv_recv, qkv_flat, 2)

    head_mask = lax.shift_right_logical(iota((HEADS_PAD, D), 1), 6) == iota((HEADS_PAD, D), 0)
    stat_row = iota((HEADS_PAD, 128), 0)
    stat_column = iota((HEADS_PAD, 128), 1)
    stat_lane = stat_column == stat_row
    stat_lane1 = stat_column == stat_row + HEADS_PAD
    stat_lane2 = stat_column == stat_row + 2 * HEADS_PAD
    stat_any = stat_lane | stat_lane1 | stat_lane2
    scaling = qk_ref[...][None, :]
    score_scale = float(DH) ** 0.5

    def heads(row):
        masked = jnp.where(head_mask, jnp.broadcast_to(row, (HEADS_PAD, D)), 0.0)
        squares = jnp.sum(masked * masked, axis=1, keepdims=True)
        return (masked * lax.rsqrt(squares + EPSILON) * scaling).astype(BF16)

    home = lax.rem(my_group + offset1, N)
    partner_here = jnp.bitwise_xor(home, pair_bits[0, 0])
    for j in range(2):
        queries = heads(qkv_flat[j : j + 1, 0:D])
        new_keys = heads(qkv_flat[j : j + 1, D : 2 * D])
        new_values = qkv_flat[j : j + 1, 2 * D : 3 * D]
        scores = sum(
            times_transposed(
                queries[:, WIDE * part : WIDE * part + WIDE],
                packed[part, 8 * j : 8 * j + 8].reshape(128, WIDE),
            )
            for part in range(KEY_PARTS)
        )
        scores = score_scale * scores
        fresh = score_scale * jnp.sum(
            queries.astype(F32) * new_keys.astype(F32), axis=1, keepdims=True
        )
        if j == 1:
            counted = jnp.full((HEADS_PAD, 1), home, jnp.int32) < partner_here
        else:
            counted = jnp.full((HEADS_PAD, 1), True)
        valid = jnp.broadcast_to(lane.astype(F32) < live2[j : j + 1, :], (HEADS_PAD, 128))
        highest = jnp.maximum(
            jnp.max(jnp.where(valid, scores, NEGATIVE), axis=1, keepdims=True),
            jnp.where(counted, fresh, NEGATIVE),
        )
        soft = jnp.where(valid, jnp.exp(jnp.where(valid, scores - highest, 0.0)), 0.0)
        fresh_weight = jnp.where(counted, jnp.exp(fresh - highest), 0.0)
        weight_sum = jnp.sum(soft, axis=1, keepdims=True) + fresh_weight
        fresh_low = fresh_weight.astype(BF16).astype(F32)
        for part in range(KEY_PARTS):
            columns = slice(WIDE * part, WIDE * part + WIDE)
            values = packed[KEY_PARTS + part, 8 * j : 8 * j + 8].reshape(128, WIDE)
            weighted = jnp.dot(soft.astype(BF16), values, preferred_element_type=F32)
            weighted = weighted + fresh_low * new_values[:, columns]
            partial_wide[j : j + 1, columns] = jnp.sum(
                jnp.where(head_mask[:, columns], weighted / weight_sum, 0.0),
                axis=0,
                keepdims=True,
            )
    total = highest + jnp.log(weight_sum)
    piece0 = total.astype(BF16).astype(F32)
    piece1 = (total - piece0).astype(BF16).astype(F32)
    piece2 = total - piece0 - piece1
    pieces = jnp.where(stat_lane, piece0, 0.0)
    pieces = pieces + jnp.where(stat_lane1, piece1, 0.0)
    pieces = pieces + jnp.where(stat_lane2, piece2, 0.0)
    partial_wide[0:1, D : D + 128] = jnp.zeros((1, 128), F32)
    partial_wide[1:2, D : D + 128] = jnp.sum(pieces, axis=0, keepdims=True)
    partial[0] = partial_wide[...].astype(BF16)

    gather_group(partial, 3)

    for part in range(3):
        deliver_cache(part)

    relay_group(partial, 3, 9)
    partner = jnp.bitwise_xor(my_group, pair_bits[0, 0])
    mine = partial[slot_of(my_group - offset1)].astype(F32)[1:2, :]
    other = partial[slot_of(partner - offset1)].astype(F32)[1:2, :]

    def total_of(row):
        pieces = jnp.broadcast_to(row[:, D : D + 128], (HEADS_PAD, 128))
        return jnp.sum(jnp.where(stat_any, pieces, 0.0), axis=1, keepdims=True)

    def by_column(column):
        return jnp.sum(jnp.where(head_mask, column, 0.0), axis=0, keepdims=True)

    my_total = total_of(mine)
    other_total = total_of(other)
    merged = jnp.maximum(my_total, other_total)
    my_factor = jnp.exp(my_total - merged)
    other_factor = jnp.exp(other_total - merged)
    both = my_factor + other_factor
    long_row = mine[:, 0:D] * by_column(my_factor / both) + other[:, 0:D] * by_column(
        other_factor / both
    )
    short_row = partial[slot_of(my_group - offset0)].astype(F32)[0:1, 0:D]
    attended = jnp.where(
        first, jnp.broadcast_to(short_row, (2, D)), jnp.broadcast_to(long_row, (2, D))
    )
    attended_rows[0] = attended.astype(BF16)
    gather(attended_rows, shard_peer, 4)
    deliver_cache(3)

    loads[3].wait()
    wait_for(others(attended_rows), recv_sem.at[4])
    spread_back(stack(attended_rows), w_out[...], 80, 256, out_send, out_recv, out_flat, 5)
    attention_out = out_flat[:, 0:D]
    mixed = rms_normal(
        own_tokens + attn_rate_ref[...][None, :] * (rms_normal(attention_out) - own_tokens)
    )
    mixed_rows[0] = mixed.astype(BF16)
    gather(mixed_rows, shard_peer, 6)

    loads[4].wait()
    loads[5].wait()
    loads[6].wait()
    wait_for(others(mixed_rows), recv_sem.at[6])
    rows = stack(mixed_rows)
    up = times_transposed(rows, w_up[...]) * up_scale_ref[...][None, :]
    gate = times_transposed(rows, w_gate[...]) * (
        gate_scale_ref[...][None, :] * float(D) ** 0.5
    )
    inner = (up * (gate / (1.0 + jnp.exp(-gate)))).astype(BF16)
    sum_wide[...] = jnp.dot(inner, w_down[...], preferred_element_type=F32)
    for k in range(N):
        sum_send[k] = sum_wide[2 * k : 2 * k + 2, :].astype(BF16)
    sum_recv[0] = sum_send[0]
    give_back(sum_send, sum_recv, 7)
    wait_for(others(sum_recv), recv_sem.at[7])
    mlp_out = sum_recv[0].astype(F32)
    for k in range(1, N):
        mlp_out = mlp_out + sum_recv[k].astype(F32)
    hidden_out[...] = rms_normal(
        mixed + mlp_rate_ref[...][None, :] * (rms_normal(mlp_out) - mixed)
    ).astype(BF16)

    for part in range(PARTS):
        wait_for(others(staged.at[part]), recv_sem.at[HOPS + PARTS + part])
        own_chunks[part].wait()
    half = pl.ds(N // 2, N // 2)
    most = pl.ds(1, N // 2 - 1)
    sent = (
        [
            piece_recv.at[pl.ds(1, PIECES - 1)],
            others(shard_rows),
            others(qkv_recv),
            partial.at[most],
            others(attended_rows),
            others(out_recv),
            others(mixed_rows),
            others(sum_recv),
            others(turn_recv),
            partial.at[half],
        ]
        + [others(arrived[part]) for part in range(PARTS)]
        + [others(staged.at[part]) for part in range(PARTS)]
    )
    for hop, ref in enumerate(sent):
        wait_for(ref, send_sem.at[hop])


def finish_kernel(hidden, cache, hidden_out, cache_out, sems):
    copies = [pltpu.make_async_copy(hidden, hidden_out, sems.at[0])]
    for number in range(8):
        part = (number // 4, pl.ds(32 * (number % 4), 32))
        copies.append(
            pltpu.make_async_copy(cache.at[part], cache_out.at[part], sems.at[1 + number])
        )
    for copy in copies:
        copy.start()
    for copy in copies:
        copy.wait()


def per_device(
    tokens,
    kv_cache,
    keep_list,
    lengths,
    merge_index,
    merge_table,
    move_offset,
    pair_mask,
    w_qkv,
    w_out,
    w_up,
    w_gate,
    w_down,
    qk_scale,
    attn_rate,
    mlp_rate,
    up_scale,
    gate_scale,
):
    vmem = pl.BlockSpec(memory_space=pltpu.VMEM)
    hbm = pl.BlockSpec(memory_space=pltpu.HBM)

    hidden, cache = pl.pallas_call(
        layer_kernel,
        out_shape=(
            pltpu.VMEM((2, D), BF16),
            pltpu.VMEM((2, 128, 2 * D), BF16),
        ),
        in_specs=[hbm] * 18,
        out_specs=(vmem, pl.BlockSpec(memory_space=pl.ANY)),
        scratch_shapes=[
            pltpu.SMEM((2,), jnp.int32),
            pltpu.SMEM((1, 2), jnp.int32),
            pltpu.SMEM((1, 1), jnp.int32),
            pltpu.VMEM((2, 128), jnp.int32),
            pltpu.VMEM((2, 128), jnp.int32),
            pltpu.VMEM((1, WTAB), BF16),
            pltpu.VMEM((D,), F32),
            pltpu.VMEM((D,), F32),
            pltpu.VMEM((D,), F32),
            pltpu.VMEM((320,), F32),
            pltpu.VMEM((320,), F32),
            pltpu.VMEM((2, 128, 2 * D), BF16),
            pltpu.VMEM((240, D), BF16),
            pltpu.VMEM((80, D), BF16),
            pltpu.VMEM((320, D), BF16),
            pltpu.VMEM((320, D), BF16),
            pltpu.VMEM((320, D), BF16),
            pltpu.VMEM((PARTS, N, 16, WIDE), BF16),
            [pltpu.VMEM((N, 16, WIDE), BF16)] * PARTS,
            pltpu.VMEM((PARTS, N, 16, WIDE), BF16),
            pltpu.VMEM((2, D), BF16),
            pltpu.VMEM((PIECES, 2, 128), BF16),
            pltpu.VMEM((PIECES, 2, 128), BF16),
            pltpu.VMEM((N, 2, 128), BF16),
            pltpu.VMEM((N, 2, 128), BF16),
            pltpu.VMEM((N, 2, D), BF16),
            pltpu.VMEM((2 * N, D), F32),
            pltpu.VMEM((N, 2, 384), F32),
            pltpu.VMEM((N, 2, 384), F32),
            pltpu.VMEM((2, 3 * D + 128), F32),
            pltpu.VMEM((2, D + 128), F32),
            pltpu.VMEM((N, 2, D + 128), BF16),
            pltpu.VMEM((N, 2, D), BF16),
            pltpu.VMEM((N, 2, 256), F32),
            pltpu.VMEM((N, 2, 256), F32),
            pltpu.VMEM((2, D + 128), F32),
            pltpu.VMEM((N, 2, D), BF16),
            pltpu.VMEM((2 * N, D), F32),
            pltpu.VMEM((N, 2, D), BF16),
            pltpu.VMEM((N, 2, D), BF16),
            pltpu.SemaphoreType.DMA((19 + PARTS,)),
            pltpu.SemaphoreType.DMA((HOPS + 2 * PARTS,)),
            pltpu.SemaphoreType.DMA((HOPS + 2 * PARTS,)),
        ],
        compiler_params=pltpu.CompilerParams(
            collective_id=0, has_side_effects=True, vmem_limit_bytes=60 << 20
        ),
    )(
        lengths,
        move_offset,
        pair_mask[None, :],
        keep_list,
        merge_index,
        merge_table[None, :],
        qk_scale,
        attn_rate,
        mlp_rate,
        up_scale,
        gate_scale,
        tokens,
        kv_cache,
        w_qkv.T,
        w_out.T,
        w_up.T,
        w_gate.T,
        w_down,
    )
    return pl.pallas_call(
        finish_kernel,
        out_shape=(
            pltpu.HBM((2, D), BF16),
            pltpu.HBM((2, 128, 2 * D), BF16),
        ),
        in_specs=[pl.BlockSpec(memory_space=pl.ANY)] * 2,
        out_specs=(pl.BlockSpec(memory_space=pl.ANY),) * 2,
        scratch_shapes=[pltpu.SemaphoreType.DMA((9,))],
    )(
        pltpu.with_memory_space_constraint(hidden, pltpu.VMEM),
        pltpu.with_memory_space_constraint(cache, pltpu.VMEM),
    )


def solution(mesh):
    return jax.shard_map(
        per_device,
        mesh=mesh,
        in_specs=(
            P(("group", "shard"), None),
            P(("group", "shard"), None, None),
            P(("group", "shard"), None),
            P(("group", "shard")),
            P(("group", "shard"), None),
            P(),
            P("shard", None),
            P("shard"),
            P(None, "shard"),
            P(None, "shard"),
            P(None, "shard"),
            P(None, "shard"),
            P("shard", None),
            P(),
            P(),
            P(),
            P("shard"),
            P("shard"),
        ),
        out_specs=(P(("group", "shard"), None), P(("group", "shard"), None, None)),
        check_vma=False,
    )
```
